512 devices in a mesh: crop: 4 (over y), space: 128 (over x, z, core).
Axes of the slice: x: 4, y: 4, z: 16, core: 2. Of those that a mesh axis runs over, the one named last changes fastest.
Arguments:
- features: bfloat16 [2048, 8, 8, 192], P(('crop', 'space')), parts along dimension 0, may hold values from -6 to 6
- cotangent: bfloat16 [2048, 8, 8, 192], P(('crop', 'space')), parts along dimension 0, may hold values from -6 to 6
- kernel: float32 [7, 7, 7, 192], replicated, may hold values from -0.3125 to 0.3125
- b_dw: float32 [192], replicated, may hold values from -3 to 3
- ln_gain: float32 [192], replicated, may hold values from 0.5 to 1.5
- ln_bias: float32 [192], replicated, may hold values from -3 to 3
- w_in_t: bfloat16 [768, 192], P('space'), may hold values from -0.4375 to 0.4375
- b_in: bfloat16 [768], P('space'), may hold values from -3 to 3
- w_out: bfloat16 [768, 192], P('space'), may hold values from -0.21875 to 0.21875
- b_out: float32 [192], replicated, may hold values from -3 to 3
- gamma: float32 [192], replicated, may hold values from 0.5 to 1.5
Outputs:
- block_out: bfloat16 [2048, 8, 8, 192], P(('crop', 'space')), parts along dimension 0
- d_x: bfloat16 [2048, 8, 8, 192], P(('crop', 'space')), parts along dimension 0
- d_kernel: float32 [28, 7, 7, 192], P('crop'), parts along dimension 0
- d_b_dw: float32 [768], P('crop'), parts along dimension 0
- d_ln_gain: float32 [768], P('crop'), parts along dimension 0
- d_ln_bias: float32 [768], P('crop'), parts along dimension 0
- d_w_in: float32 [3072, 192], P(('crop', 'space')), parts along dimension 0
- d_b_in: float32 [3072], P(('crop', 'space')), parts along dimension 0
- d_w_out: float32 [3072, 192], P(('crop', 'space')), parts along dimension 0
- d_b_out: float32 [768], P('crop'), parts along dimension 0
- d_gamma: float32 [768], P('crop'), parts along dimension 0
The draws below stay inside these ranges and needn't reach their ends.
There are 4 independent parts, one for each index of `crop`. The reference program is written for one: setup_inputs(seed, part) draws one part's arguments, and reference() takes and returns one part's arrays. A program takes and returns all parts, laid end to end along the dimension named above; an argument that names none is the same for every part. Nothing has to cross between parts.
All inputs are finite; a program needn't handle non-finite values.
Results may differ from the reference program's by a relative error of at most 0.0065.
Values may be sent and summed in bfloat16 or wider, within the bound.
A program may use at most 64 MiB of HBM per device.

```python
import jax
import jax.numpy as jnp
from jax import lax

C = 192
H = 768
KS = 7
SLAB = 4
GY = 8
GZ = 8
GX = 512


def shard_levels(own_key, shape, split, least, largest):
    level, own = 1.0, jax.random.fold_in(own_key, 6)
    for position, parts in split:
        draws = jnp.exp(jax.random.uniform(jax.random.fold_in(own, position), (parts,), jnp.float32, least / len(split), largest / len(split)))
        level = level * jnp.repeat(draws, shape[position] // parts).reshape([-1 if axis == position else 1 for axis in range(len(shape))])
    return level


def noise(rng, extent, deviation, most, pieces=(), held_as=jnp.bfloat16):
    array = jax.random.normal(rng, extent, jnp.float32) * deviation
    if len(pieces) > 0:
        array = shard_levels(rng, extent, pieces, -0.22, 0.18) * array
    return jnp.clip(array, min=-most, max=most).astype(held_as)


def setup_inputs(seed: int = 0, part: int = 0) -> dict:
    key_list = jax.random.split(jax.random.key(seed), 12)
    part_splits = jax.random.split(jax.random.fold_in(key_list[11], part), 12)
    features = noise(part_splits[0], (GX, GY, GZ, C), 1.0, 6.0, ((0, 128),))
    cotangent = noise(part_splits[1], (GX, GY, GZ, C), 1.0, 6.0, ((0, 128),))
    kernel = noise(key_list[2], (KS, KS, KS, C), (KS * KS * KS) ** -0.5, 0.3125, (), jnp.float32)
    b_dw = noise(key_list[3], (C,), 0.5, 3.0, (), jnp.float32)
    ln_gain = jnp.clip(jax.random.uniform(key_list[4], (C,), jnp.float32, 0.5, 1.5), 0.5, 1.5)
    ln_bias = noise(key_list[5], (C,), 0.5, 3.0, (), jnp.float32)
    w_in_t = noise(key_list[6], (H, C), C ** -0.5, 0.4375, ((0, 128),))
    b_in = noise(key_list[7], (H,), 0.5, 3.0, ((0, 128),))
    w_out = noise(key_list[8], (H, C), H ** -0.5, 0.21875, ((0, 128),))
    b_out = noise(key_list[9], (C,), 0.5, 3.0, (), jnp.float32)
    gamma = jnp.clip(jax.random.uniform(key_list[10], (C,), jnp.float32, 0.5, 1.5), 0.5, 1.5)
    return {"features": features, "cotangent": cotangent, "kernel": kernel, "b_dw": b_dw, "ln_gain": ln_gain, "ln_bias": ln_bias, "w_in_t": w_in_t, "b_in": b_in, "w_out": w_out, "b_out": b_out, "gamma": gamma}


root_half = 0.7071067811865476
inv_root_tau = 0.3989422804014327

def gelu_value(pre):
    return 0.5 * pre * (1.0 + lax.erf(pre * root_half))

def gelu_slope(pre):
    return 0.5 * (1.0 + lax.erf(pre * root_half)) + pre * jnp.exp(-0.5 * pre * pre) * inv_root_tau

def stencil(padded, kernel, size_x, size_y, size_z):
    width = kernel.shape[0]
    total = jnp.zeros((size_x, size_y, size_z, padded.shape[3]), jnp.float32)
    for along_x in range(width):
        for along_y in range(width):
            for along_z in range(width):
                window = padded[along_x:along_x + size_x, along_y:along_y + size_y, along_z:along_z + size_z]
                total = total + window.astype(jnp.float32) * kernel[along_x, along_y, along_z]
    return total

def kernel_terms(padded, grad, width):
    size_x, size_y, size_z, chans = grad.shape
    grad_f = grad.astype(jnp.float32)
    terms = []
    for along_x in range(width):
        for along_y in range(width):
            for along_z in range(width):
                window = padded[along_x:along_x + size_x, along_y:along_y + size_y, along_z:along_z + size_z]
                terms.append(lax.optimization_barrier(jnp.sum(window.astype(jnp.float32) * grad_f, axis=(0, 1, 2))))
    return jnp.stack(terms).reshape(width, width, width, chans)

def reference(features, cotangent, kernel, b_dw, ln_gain, ln_bias, w_in_t, b_in, w_out, b_out, gamma):
    size_x, size_y, size_z, chans = features.shape
    width = kernel.shape[0]
    half = width // 2
    scale = float(size_x * size_y * size_z) ** (-0.5)
    padded = jnp.pad(features, ((half, half), (half, half), (half, half), (0, 0)))
    mixed = stencil(padded, kernel, size_x, size_y, size_z) + b_dw
    centred = mixed - lax.optimization_barrier(jnp.mean(mixed, axis=-1, keepdims=True))
    inverse = lax.rsqrt(lax.optimization_barrier(jnp.mean(centred * centred, axis=-1, keepdims=True)) + 1e-06)
    unit_value = centred * inverse
    normed = (unit_value * ln_gain + ln_bias).astype(jnp.bfloat16)
    block_rows = SLAB * GY * GZ
    blocks = size_x * size_y * size_z // block_rows
    normed_b = normed.reshape(blocks, block_rows, chans)
    input_b = features.reshape(blocks, block_rows, chans)
    cot_b = cotangent.reshape(blocks, block_rows, chans)
    hidden_units = w_in_t.shape[0]
    b_in_f = b_in.astype(jnp.float32)

    def one_block(carry, items):
        acc_wi, acc_bi, acc_wo, acc_bo, acc_gm = carry
        normed_rows, input_rows, cot_rows = items
        pre = lax.dot_general(normed_rows, w_in_t, (((1,), (1,)), ((), ())), preferred_element_type=jnp.float32) + b_in_f
        hidden = gelu_value(pre).astype(jnp.bfloat16)
        branch = jnp.dot(hidden, w_out, preferred_element_type=jnp.float32) + b_out
        output = (input_rows.astype(jnp.float32) + gamma * branch).astype(jnp.bfloat16)
        cot_f = cot_rows.astype(jnp.float32)
        d_branch = gamma * cot_f
        d_branch_b = d_branch.astype(jnp.bfloat16)
        d_hidden = lax.dot_general(d_branch_b, w_out, (((1,), (1,)), ((), ())), preferred_element_type=jnp.float32)
        d_pre = d_hidden * gelu_slope(pre)
        d_pre_b = d_pre.astype(jnp.bfloat16)
        d_normed = jnp.dot(d_pre_b, w_in_t, preferred_element_type=jnp.float32)
        acc_wo = acc_wo + lax.dot_general(hidden, d_branch_b, (((0,), (0,)), ((), ())), preferred_element_type=jnp.float32)
        acc_wi = acc_wi + lax.dot_general(d_pre_b, normed_rows, (((0,), (0,)), ((), ())), preferred_element_type=jnp.float32)
        acc_bi = acc_bi + lax.optimization_barrier(jnp.sum(d_pre, axis=0))
        acc_bo = acc_bo + lax.optimization_barrier(jnp.sum(d_branch, axis=0))
        acc_gm = acc_gm + lax.optimization_barrier(jnp.sum(cot_f * branch, axis=0))
        return ((acc_wi, acc_bi, acc_wo, acc_bo, acc_gm), (output, d_normed))
    start = (jnp.zeros((hidden_units, chans), jnp.float32), jnp.zeros((hidden_units,), jnp.float32), jnp.zeros((hidden_units, chans), jnp.float32), jnp.zeros((chans,), jnp.float32), jnp.zeros((chans,), jnp.float32))
    sums, outs = lax.scan(one_block, start, (normed_b, input_b, cot_b))
    acc_wi, acc_bi, acc_wo, acc_bo, acc_gm = sums
    output = outs[0].reshape(size_x, size_y, size_z, chans)
    d_normed = outs[1].reshape(size_x, size_y, size_z, chans)
    d_ln_gain = lax.optimization_barrier(jnp.sum(d_normed * unit_value, axis=(0, 1, 2)))
    d_ln_bias = lax.optimization_barrier(jnp.sum(d_normed, axis=(0, 1, 2)))
    scaled = d_normed * ln_gain
    d_mixed = inverse * (scaled - lax.optimization_barrier(jnp.mean(scaled, axis=-1, keepdims=True)) - unit_value * lax.optimization_barrier(jnp.mean(scaled * unit_value, axis=-1, keepdims=True)))
    d_b_dw = lax.optimization_barrier(jnp.sum(d_mixed, axis=(0, 1, 2)))
    d_mixed_b = d_mixed.astype(jnp.bfloat16)
    d_kernel = kernel_terms(padded, d_mixed_b, width)
    grad_pad = jnp.pad(d_mixed_b, ((half, half), (half, half), (half, half), (0, 0)))
    back = stencil(grad_pad, kernel[::-1, ::-1, ::-1], size_x, size_y, size_z)
    d_x = (cotangent.astype(jnp.float32) + back).astype(jnp.bfloat16)
    return (output, d_x, d_kernel * scale, d_b_dw * scale, d_ln_gain * scale, d_ln_bias * scale, acc_wi * scale, acc_bi * scale, acc_wo * scale, acc_bo * scale, acc_gm * scale)
```

```python
import numpy as np
import jax
import jax.numpy as jnp
import ml_dtypes
from jax import lax
from jax.experimental import pallas as pl
from jax.experimental.pallas import tpu as pltpu
from jax.sharding import PartitionSpec as P

root_half = 0.7071067811865476
inv_root_tau = 0.3989422804014327
MESH = pl.DeviceIdType.MESH
F32 = jnp.float32
BF = jnp.bfloat16

NX, NZ, NS = 4, 16, 128
C = 192
W = 7
G = 8
SX = 4
CELLS = SX * G * G
N = 11
NF = 64
UNITS = 6
LANES = 512
GROUPS = 7
TILES = 2 * GROUPS


def split_np(m):
    high = m.astype(ml_dtypes.bfloat16)
    low = (m - high.astype(np.float64)).astype(ml_dtypes.bfloat16)
    return high, low


def transforms():
    seen, reps = set(), []
    for u in range(N):
        for v in range(N):
            if (u, v) in seen:
                continue
            reps.append((u, v))
            seen.add((u, v))
            seen.add(((-u) % N, (-v) % N))
    u = np.array([r[0] for r in reps])[:, None]
    v = np.array([r[1] for r in reps])[:, None]
    weight = np.where((u == 0) & (v == 0), 1.0, 2.0) / N**2
    n = len(reps)

    def table(pos_j, pos_k, live, sign):
        angle = 2 * np.pi / N * (u * pos_j[None] + v * pos_k[None])
        out = np.zeros((2 * NF, len(pos_j)))
        out[:n] = np.cos(angle) * live
        out[NF : NF + n] = sign * np.sin(angle) * live
        return out

    scale = np.zeros((2 * NF, 1))
    scale[:n] = weight
    scale[NF : NF + n] = weight
    cell = np.arange(G * G)
    tap = np.arange(8 * W)
    live = ((tap % 8) < W)[None]
    fwd = table(cell // G, cell % G, 1.0, -1.0)
    inv = (fwd * scale).T
    ker = table(tap // 8 - 3, tap % 8 - 3, live, 1.0)
    lag = (table(tap // 8 - 3, tap % 8 - 3, live, -1.0) * scale).T
    fm = np.concatenate(split_np(fwd), axis=0)
    return fm, np.stack(split_np(ker)), np.stack(split_np(inv)), np.stack(split_np(lag))


def dot(a, b):
    return jnp.dot(a, b, preferred_element_type=F32)


def dot_nt(a, b):
    return lax.dot_general(a, b, (((1,), (1,)), ((), ())), preferred_element_type=F32)


def dot_tn(a, b):
    return lax.dot_general(a, b, (((0,), (0,)), ((), ())), preferred_element_type=F32)


def halves(value):
    high = value.astype(BF)
    return high, (value - high.astype(F32)).astype(BF)


def dot3(m, value):
    high, low = halves(value)
    return dot(m[0], high) + dot(m[1], high) + dot(m[0], low)


def kernel_body(
    x_ref, cot_ref, ker_ref, bdw_ref, gain_ref, bias_ref, blk_ref, bout_ref, gamma_ref,
    fm_ref, km_ref, im_ref, lm_ref,
    out_ref, dx_ref, dker_ref, vec_ref, dwi_ref, dwo_ref, dbi_ref,
    halo_x, halo_d, wall, swall, r1, t1, t1b, r2, t2, t2b, r3,
    kpad, kf, xf, df, yf, gf, mixed, na, dba, branch, dnorm, dmb,
    pay, payb, rx, zt, ztb, rz, agz, fin,
    s_halo, q_halo, s_ga, q_ga, s_gb, q_gb, s_gc, q_gc, s_hd, q_hd,
    s_rc, q_rc, s_rb, q_rb, s_ra, q_ra, s_px, q_px, s_pz, q_pz, s_az, q_az, s_ax, q_ax,
):
    scale = float(NS * CELLS) ** (-0.5)
    s = lax.axis_index("space")
    core = lax.rem(s, 2)
    z = lax.rem(s // 2, NZ)
    x = s // (2 * NZ)

    def place(px, pz, pc):
        return {"space": (px * NZ + pz) * 2 + pc}

    def at_z(d):
        return place(x, lax.rem(z + d + NZ, NZ), core)

    def at_x(d):
        return place(lax.rem(x + d + NX, NX), z, core)

    def at_xc(k):
        return place(lax.rem(x + k % NX, NX), z, core if k < NX else 1 - core)

    partner = place(x, z, 1 - core)
    right = {"space": lax.rem(s + 1, NS)}
    left = {"space": lax.rem(s + NS - 1, NS)}

    def copy(src, dst, ssem, rsem, dev):
        return pltpu.make_async_remote_copy(
            src_ref=src, dst_ref=dst, send_sem=ssem, recv_sem=rsem, device_id=dev, device_id_type=MESH
        )

    pending = []

    def launch(copies):
        for c in copies:
            c.start()
        pending.extend(copies)
        return copies

    def arrive(copies):
        for c in copies:
            c.wait_recv()

    barrier = pltpu.get_barrier_semaphore()
    peers = [at_z(d) for d in range(1, NZ)] + [at_xc(k) for k in range(1, 2 * NX)] + [left, right]
    for dev in peers:
        pl.semaphore_signal(barrier, inc=1, device_id=dev, device_id_type=MESH)
    pl.semaphore_wait(barrier, len(peers))

    halo = launch([
        copy(x_ref.at[pl.ds(64, 192)], halo_x.at[0], s_halo.at[0], q_halo.at[0], right),
        copy(x_ref.at[pl.ds(0, 192)], halo_x.at[1], s_halo.at[1], q_halo.at[1], left),
    ])
    gather_a = launch([
        copy(blk_ref, wall.at[0, 0, d], s_ga.at[d - 1], q_ga.at[d - 1], at_z(d)) for d in range(1, NZ)
    ])
    wall[0, 0, 0] = blk_ref[...]

    kpad[...] = jnp.zeros_like(kpad)
    for a in range(W):
        for b in range(W):
            kpad[a, 8 * b : 8 * b + W, :] = ker_ref[a, b]

    def transform(rows):
        both = dot(fm_ref[...], rows)
        return both[: 2 * NF] + both[2 * NF :]

    km = (km_ref[0], km_ref[1])

    def ker_step(a, carry):
        kf[a] = dot3(km, kpad[a])
        return carry

    lax.fori_loop(0, W, ker_step, 0)
    for p in range(SX):
        xf[3 + p] = transform(x_ref[64 * p : 64 * p + 64, :])

    arrive(gather_a)
    gather_b = launch([
        copy(wall.at[0, 0], wall.at[0, d], s_gb.at[d - 1], q_gb.at[d - 1], at_x(d)) for d in range(1, NX)
    ])

    arrive(halo)
    has_left = (s > 0).astype(F32)
    has_right = (s < NS - 1).astype(F32)
    for p in range(3):
        xf[p] = transform(halo_x[0, 64 * p : 64 * p + 64, :]) * has_left
        xf[7 + p] = transform(halo_x[1, 64 * p : 64 * p + 64, :]) * has_right

    def forward_step(g, carry):
        top, low = pl.ds(pl.multiple_of(8 * g, 8), 8), pl.ds(pl.multiple_of(8 * g + NF, 8), 8)
        re = jnp.zeros((SX, 8, C), F32)
        im = jnp.zeros((SX, 8, C), F32)
        for a in range(W):
            kr, ki = kf[a, top, :], kf[a, low, :]
            xr, xi = xf[a : a + SX, top, :], xf[a : a + SX, low, :]
            re = re + kr * xr - ki * xi
            im = im + kr * xi + ki * xr
        yf[:, top, :] = re
        yf[:, low, :] = im
        return carry

    lax.fori_loop(0, NF // 8, forward_step, 0)
    inv = (im_ref[0], im_ref[1])
    for p in range(SX):
        mixed[64 * p : 64 * p + 64, :] = dot3(inv, yf[p]) + bdw_ref[...]

    arrive(gather_b)
    gather_c = launch([copy(wall.at[0], wall.at[1], s_gc.at[0], q_gc.at[0], partner)])

    mix = mixed[...]
    centred = mix - jnp.mean(mix, axis=-1, keepdims=True)
    inverse = lax.rsqrt(jnp.mean(centred * centred, axis=-1, keepdims=True) + 1e-06)
    unit = centred * inverse
    mixed[...] = unit
    lane = lax.broadcasted_iota(jnp.int32, (CELLS, 128), 1)
    na[:, 128:256] = jnp.where(lane == C - 128, 1.0, 0.0).astype(BF)
    na[:, 0:C] = (unit * gain_ref[...] + bias_ref[...]).astype(BF)
    dba[:, 128:256] = jnp.zeros((CELLS, 128), BF)
    dba[:, 0:C] = (gamma_ref[...] * cot_ref[...].astype(F32)).astype(BF)
    branch[...] = jnp.zeros_like(branch)
    dnorm[...] = jnp.zeros_like(dnorm)

    def units(dc):
        def chunk(i, carry):
            two = pl.ds(2 * i, 2)
            rows = wall[dc, two].astype(F32).reshape(256, LANES).astype(BF)
            win, wout = rows[:, 0:256], rows[:, 256:512]
            normed, db = na[...], dba[...]
            pre = dot_nt(normed, win)
            half_erf = 0.5 * (1.0 + lax.erf(pre * root_half))
            hidden = (pre * half_erf).astype(BF)
            slope = half_erf + pre * jnp.exp(-0.5 * pre * pre) * inv_root_tau
            branch[...] += dot(hidden, wout)
            d_pre = (dot_nt(db, wout) * slope).astype(BF)
            dnorm[...] += dot(d_pre, win)
            dwi = (dot_tn(d_pre, normed) * scale).reshape(2, NZ, 8, 256)
            dwo = (dot_tn(hidden, db) * scale).reshape(2, NZ, 8, 256)
            if dc == 0:
                t1[two, :, :, 0:256] = dwi
                t1[two, :, :, 256:512] = dwo
            else:
                swall[two, :, :, 0:256] = dwi.astype(BF)
                swall[two, :, :, 256:512] = dwo.astype(BF)
            return carry

        lax.fori_loop(0, 2, chunk, 0)

    units(0)
    arrive(gather_c)
    units(1)
    scatter_c = launch([copy(swall, r1, s_rc.at[0], q_rc.at[0], partner)])

    cot = cot_ref[...].astype(F32)
    full = branch[:, 0:C] + bout_ref[...]
    out_ref[...] = (x_ref[...].astype(F32) + gamma_ref[...] * full).astype(BF)
    v_gamma = jnp.sum(cot * full, axis=0, keepdims=True)
    v_bout = jnp.sum(gamma_ref[...] * cot, axis=0, keepdims=True)

    dn = dnorm[:, 0:C]
    unit2 = mixed[...]
    v_gain = jnp.sum(dn * unit2, axis=0, keepdims=True)
    v_bias = jnp.sum(dn, axis=0, keepdims=True)
    scaled = dn * gain_ref[...]
    d_mixed = inverse * (
        scaled
        - jnp.mean(scaled, axis=-1, keepdims=True)
        - unit2 * jnp.mean(scaled * unit2, axis=-1, keepdims=True)
    )
    v_bdw = jnp.sum(d_mixed, axis=0, keepdims=True)
    dmb[...] = d_mixed.astype(BF)
    halo2 = launch([
        copy(dmb.at[pl.ds(64, 192)], halo_d.at[0], s_hd.at[0], q_hd.at[0], right),
        copy(dmb.at[pl.ds(0, 192)], halo_d.at[1], s_hd.at[1], q_hd.at[1], left),
    ])
    for p in range(SX):
        df[3 + p] = transform(dmb[64 * p : 64 * p + 64, :])

    def grad_step(g, carry):
        top, low = pl.ds(pl.multiple_of(8 * g, 8), 8), pl.ds(pl.multiple_of(8 * g + NF, 8), 8)
        dr, di = df[3 : 3 + SX, top, :], df[3 : 3 + SX, low, :]
        for a in range(W):
            xr, xi = xf[a : a + SX, top, :], xf[a : a + SX, low, :]
            gf[a, top, :] = jnp.sum(dr * xr + di * xi, axis=0)
            gf[a, low, :] = jnp.sum(dr * xi - di * xr, axis=0)
        return carry

    lax.fori_loop(0, NF // 8, grad_step, 0)
    lag = (lm_ref[0], lm_ref[1])
    pay[...] = jnp.zeros_like(pay)
    vectors = [v_bdw, v_gain, v_bias, v_bout, v_gamma]
    for a in range(W):
        taps = dot3(lag, gf[a]) * scale
        for b in range(W):
            group = a * W + b
            block = taps[8 * b : 8 * b + 8, :]
            q, t = group // GROUPS, 2 * (group % GROUPS)
            pay[q, t] = block[:, 0:128]
            pay[q, t + 1, :, 0 : C - 128] = block[:, 128:C]
    for i, v in enumerate(vectors):
        pay[0, 2 * i, W : W + 1, :] = v[:, 0:128] * scale
        pay[0, 2 * i + 1, W : W + 1, 0 : C - 128] = v[:, 128:C] * scale
    payb[...] = pay[...].astype(BF)

    def chunk_of(k):
        px = lax.rem(x + k % NX, NX)
        pc = core if k < NX else 1 - core
        return pc * NX + px

    own = chunk_of(0)
    sum_x = launch([
        copy(payb.at[chunk_of(k)], rx.at[k - 1], s_px.at[k - 1], q_px.at[k - 1], at_xc(k))
        for k in range(1, 2 * NX)
    ])

    arrive(scatter_c)

    def add_core(i, carry):
        total = t1[i] + r1[i].astype(F32)
        t1[i] = total
        t1b[i] = total.astype(BF)
        return carry

    lax.fori_loop(0, NX, add_core, 0)
    scatter_b = launch([
        copy(t1b.at[d], r2.at[d - 1], s_rb.at[d - 1], q_rb.at[d - 1], at_x(-d)) for d in range(1, NX)
    ])

    arrive(halo2)
    for p in range(3):
        df[p] = transform(halo_d[0, 64 * p : 64 * p + 64, :]) * has_left
        df[7 + p] = transform(halo_d[1, 64 * p : 64 * p + 64, :]) * has_right

    arrive(sum_x)
    total = pay[own]
    for k in range(2 * NX - 1):
        total = total + rx[k].astype(F32)
    zt[...] = total
    ztb[...] = total.astype(BF)
    sum_z = launch([
        copy(ztb.at[lax.rem(z + d, NZ)], rz.at[d - 1], s_pz.at[d - 1], q_pz.at[d - 1], at_z(d))
        for d in range(1, NZ)
    ])

    def back_step(g, carry):
        top, low = pl.ds(pl.multiple_of(8 * g, 8), 8), pl.ds(pl.multiple_of(8 * g + NF, 8), 8)
        re = jnp.zeros((SX, 8, C), F32)
        im = jnp.zeros((SX, 8, C), F32)
        for a in range(W):
            kr, ki = kf[W - 1 - a, top, :], kf[W - 1 - a, low, :]
            dr, di = df[a : a + SX, top, :], df[a : a + SX, low, :]
            re = re + kr * dr + ki * di
            im = im + kr * di - ki * dr
        yf[:, top, :] = re
        yf[:, low, :] = im
        return carry

    lax.fori_loop(0, NF // 8, back_step, 0)

    arrive(scatter_b)
    t2v = t1[0]
    for d in range(NX - 1):
        t2v = t2v + r2[d].astype(F32)
    t2[...] = t2v
    t2b[...] = t2v.astype(BF)
    scatter_a = launch([
        copy(t2b.at[d], r3.at[d - 1], s_ra.at[d - 1], q_ra.at[d - 1], at_z(-d)) for d in range(1, NZ)
    ])

    arrive(sum_z)
    tile = zt[z]
    for d in range(NZ - 1):
        tile = tile + rz[d].astype(F32)
    agz[z] = tile.astype(BF)
    gather_z = launch([
        copy(agz.at[z], agz.at[z], s_az.at[d - 1], q_az.at[d - 1], at_z(d)) for d in range(1, NZ)
    ])

    for p in range(SX):
        rows = slice(64 * p, 64 * p + 64)
        dx_ref[rows, :] = (cot_ref[rows, :].astype(F32) + dot3(inv, yf[p])).astype(BF)

    arrive(gather_z)
    fin[own] = agz[...]
    gather_x = launch([
        copy(agz, fin.at[own], s_ax.at[k - 1], q_ax.at[k - 1], at_xc(k)) for k in range(1, 2 * NX)
    ])

    arrive(scatter_a)
    mine = t2[0]
    for d in range(NZ - 1):
        mine = mine + r3[d].astype(F32)
    dwi_ref[...] = mine[0:UNITS, 0:C]
    dwo_ref[...] = mine[0:UNITS, 256 : 256 + C]
    row = lax.broadcasted_iota(jnp.int32, (8, 128), 0)
    col = lax.broadcasted_iota(jnp.int32, (8, 128), 1)
    bias_col = jnp.broadcast_to(mine[:, C : C + 1], (8, 128))
    dbi_ref[...] = jnp.sum(jnp.where(row == col, bias_col, 0.0), axis=0, keepdims=True)

    arrive(gather_x)
    for group in range(W * W):
        q, t = group // GROUPS, 2 * (group % GROUPS)
        first, second = fin[q, t].astype(F32), fin[q, t + 1].astype(F32)
        dker_ref[group // W, group % W, :, 0:128] = first[0:W]
        dker_ref[group // W, group % W, :, 128:C] = second[0:W, 0 : C - 128]
        if group < 5:
            vec_ref[group : group + 1, 0:128] = first[W : W + 1]
            vec_ref[group : group + 1, 128:C] = second[W : W + 1, 0 : C - 128]

    for c in pending:
        c.wait_send()


def on_device(
    features, cotangent, kernel, b_dw, ln_gain, ln_bias, w_in_t, b_in, w_out, b_out, gamma
):
    block = jnp.concatenate(
        [
            jnp.pad(jnp.concatenate([w_in_t, b_in[:, None]], axis=1), ((0, 2), (0, 255 - C))),
            jnp.pad(w_out, ((0, 2), (0, 256 - C))),
        ],
        axis=1,
    )
    fm, km, im, lm = (jnp.asarray(m) for m in transforms())
    vm = pl.BlockSpec(memory_space=pltpu.VMEM)
    dma = pltpu.SemaphoreType.DMA
    counts = [2, NZ - 1, NX - 1, 1, 2, 1, NX - 1, NZ - 1, 2 * NX - 1, NZ - 1, NZ - 1, 2 * NX - 1]
    sems = [dma((n,)) for n in counts for _ in range(2)]
    scratch = [
        pltpu.VMEM((2, 192, C), BF),
        pltpu.VMEM((2, 192, C), BF),
        pltpu.VMEM((2, NX, NZ, 8, LANES), BF),
        pltpu.VMEM((NX, NZ, 8, LANES), BF),
        pltpu.VMEM((NX, NZ, 8, LANES), BF),
        pltpu.VMEM((NX, NZ, 8, LANES), F32),
        pltpu.VMEM((NX, NZ, 8, LANES), BF),
        pltpu.VMEM((NX - 1, NZ, 8, LANES), BF),
        pltpu.VMEM((NZ, 8, LANES), F32),
        pltpu.VMEM((NZ, 8, LANES), BF),
        pltpu.VMEM((NZ - 1, 8, LANES), BF),
        pltpu.VMEM((W, 8 * W, C), F32),
        pltpu.VMEM((W, 2 * NF, C), F32),
        pltpu.VMEM((SX + 6, 2 * NF, C), F32),
        pltpu.VMEM((SX + 6, 2 * NF, C), F32),
        pltpu.VMEM((SX, 2 * NF, C), F32),
        pltpu.VMEM((W, 2 * NF, C), F32),
        pltpu.VMEM((CELLS, C), F32),
        pltpu.VMEM((CELLS, 256), BF),
        pltpu.VMEM((CELLS, 256), BF),
        pltpu.VMEM((CELLS, 256), F32),
        pltpu.VMEM((CELLS, 256), F32),
        pltpu.VMEM((CELLS, C), BF),
        pltpu.VMEM((2 * NX, NZ, 8, 128), F32),
        pltpu.VMEM((2 * NX, NZ, 8, 128), BF),
        pltpu.VMEM((2 * NX - 1, NZ, 8, 128), BF),
        pltpu.VMEM((NZ, 8, 128), F32),
        pltpu.VMEM((NZ, 8, 128), BF),
        pltpu.VMEM((NZ - 1, 8, 128), BF),
        pltpu.VMEM((NZ, 8, 128), BF),
        pltpu.VMEM((2 * NX, NZ, 8, 128), BF),
    ]
    out, dx, dker, vec, dwi, dwo, dbi = pl.pallas_call(
        kernel_body,
        out_shape=(
            jax.ShapeDtypeStruct((CELLS, C), BF),
            jax.ShapeDtypeStruct((CELLS, C), BF),
            jax.ShapeDtypeStruct((W, W, W, C), F32),
            jax.ShapeDtypeStruct((8, C), F32),
            jax.ShapeDtypeStruct((UNITS, C), F32),
            jax.ShapeDtypeStruct((UNITS, C), F32),
            jax.ShapeDtypeStruct((1, 128), F32),
        ),
        in_specs=[vm] * 13,
        out_specs=(vm,) * 7,
        scratch_shapes=scratch + sems,
        compiler_params=pltpu.CompilerParams(
            collective_id=0, has_side_effects=True, vmem_limit_bytes=48 * 1024 * 1024
        ),
    )(
        features.reshape(CELLS, C), cotangent.reshape(CELLS, C), kernel,
        b_dw.reshape(1, C), ln_gain.reshape(1, C), ln_bias.reshape(1, C), block,
        b_out.reshape(1, C), gamma.reshape(1, C), fm, km, im, lm,
    )
    shape = features.shape
    return (
        out.reshape(shape), dx.reshape(shape), dker,
        vec[0], vec[1], vec[2], dwi, dbi[0, 0:UNITS], dwo, vec[3], vec[4],
    )


def solution(mesh):
    cells = P(("crop", "space"), None, None, None)
    rows = P(("crop", "space"), None)
    in_specs = (
        cells, cells, P(), P(), P(), P(), P("space", None), P("space"), P("space", None), P(), P(),
    )
    out_specs = (
        cells, cells, P("crop", None, None, None), P("crop"), P("crop"), P("crop"),
        rows, P(("crop", "space")), rows, P("crop"), P("crop"),
    )
    return jax.shard_map(
        on_device, mesh=mesh, in_specs=in_specs, out_specs=out_specs, check_vma=False
    )
```

```python
import numpy as np
import jax
import jax.numpy as jnp
import ml_dtypes
from jax import lax
from jax.experimental import pallas as pl
from jax.experimental.pallas import tpu as pltpu
from jax.sharding import PartitionSpec as P

root_half = 0.7071067811865476
inv_root_tau = 0.3989422804014327
MESH = pl.DeviceIdType.MESH
F32 = jnp.float32
BF = jnp.bfloat16

NX, NZ, NS = 4, 16, 128
C = 192
W = 7
G = 8
SX = 4
CELLS = SX * G * G
N = 11
NF = 64
UNITS = 6
LANES = 384
GROUPS = 7
TILES = 2 * GROUPS


def split_np(m):
    high = m.astype(ml_dtypes.bfloat16)
    low = (m - high.astype(np.float64)).astype(ml_dtypes.bfloat16)
    return high, low


def transforms():
    seen, reps = set(), []
    for u in range(N):
        for v in range(N):
            if (u, v) in seen:
                continue
            reps.append((u, v))
            seen.add((u, v))
            seen.add(((-u) % N, (-v) % N))
    u = np.array([r[0] for r in reps])[:, None]
    v = np.array([r[1] for r in reps])[:, None]
    weight = np.where((u == 0) & (v == 0), 1.0, 2.0) / N**2
    n = len(reps)

    def table(pos_j, pos_k, live, sign):
        angle = 2 * np.pi / N * (u * pos_j[None] + v * pos_k[None])
        out = np.zeros((2 * NF, len(pos_j)))
        out[:n] = np.cos(angle) * live
        out[NF : NF + n] = sign * np.sin(angle) * live
        return out

    scale = np.zeros((2 * NF, 1))
    scale[:n] = weight
    scale[NF : NF + n] = weight
    cell = np.arange(G * G)
    tap = np.arange(8 * W)
    live = ((tap % 8) < W)[None]
    fwd = table(cell // G, cell % G, 1.0, -1.0)
    inv = (fwd * scale).T
    ker = table(tap // 8 - 3, tap % 8 - 3, live, 1.0)
    lag = (table(tap // 8 - 3, tap % 8 - 3, live, -1.0) * scale).T
    fm = np.concatenate(split_np(fwd), axis=0)
    return fm, np.stack(split_np(ker)), np.stack(split_np(inv)), np.stack(split_np(lag))


def dot(a, b):
    return jnp.dot(a, b, preferred_element_type=F32)


def dot_nt(a, b):
    return lax.dot_general(a, b, (((1,), (1,)), ((), ())), preferred_element_type=F32)


def dot_tn(a, b):
    return lax.dot_general(a, b, (((0,), (0,)), ((), ())), preferred_element_type=F32)


def halves(value):
    high = value.astype(BF)
    return high, (value - high.astype(F32)).astype(BF)


def dot3(m, value):
    high, low = halves(value)
    return dot(m[0], high) + dot(m[1], high) + dot(m[0], low)


def kernel_body(
    x_hbm, cot_hbm, ker_hbm, bdw_hbm, gain_hbm, bias_hbm, win_hbm, bin_hbm, wout_hbm, bout_hbm,
    gamma_hbm, fm_hbm, km_hbm, im_hbm, lm_hbm,
    out_ref, dx_ref, dker_ref, vbdw_ref, vgain_ref, vbias_ref, dwi_ref, dbi_ref, dwo_ref,
    vbout_ref, vgamma_ref,
    x_ref, cot_ref, ker_ref, bdw_ref, gain_ref, bias_ref, win_ref, bin_ref, wout_ref, bout_ref,
    gamma_ref, fm_ref, km_ref, im_ref, lm_ref, l_sem, blk_ref,
    halo_x, halo_d, wall, swall, r1, t1, t1b, r2, t2, t2b, r3,
    kpad, kf, xf, df, yf, gf, mixed, na, dba, branch, dnorm, dmb,
    pay, payb, rx, zt, ztb, rz, agz, fin, wrk,
    s_halo, q_halo, s_ga, q_ga, s_gb, q_gb, s_gc, q_gc, s_hd, q_hd,
    s_rc, q_rc, s_rb, q_rb, s_ra, q_ra, s_px, q_px, s_pz, q_pz, s_az, q_az, s_ax, q_ax,
):
    scale = float(NS * CELLS) ** (-0.5)
    s = lax.axis_index("space")
    core = lax.rem(s, 2)
    z = lax.rem(s // 2, NZ)
    x = s // (2 * NZ)

    def place(px, pz, pc):
        return {"space": (px * NZ + pz) * 2 + pc}

    def at_z(d):
        return place(x, lax.rem(z + d + NZ, NZ), core)

    def at_x(d):
        return place(lax.rem(x + d + NX, NX), z, core)

    def at_xc(k):
        return place(lax.rem(x + k % NX, NX), z, core if k < NX else 1 - core)

    partner = place(x, z, 1 - core)
    right = {"space": lax.rem(s + 1, NS)}
    left = {"space": lax.rem(s + NS - 1, NS)}

    def copy(src, dst, ssem, rsem, dev):
        return pltpu.make_async_remote_copy(
            src_ref=src, dst_ref=dst, send_sem=ssem, recv_sem=rsem, device_id=dev, device_id_type=MESH
        )

    pending = []

    def launch(copies):
        for c in copies:
            c.start()
        pending.extend(copies)
        return copies

    def arrive(copies):
        for c in copies:
            c.wait_recv()

    pairs = [
        (win_hbm, win_ref), (bin_hbm, bin_ref), (wout_hbm, wout_ref), (ker_hbm, ker_ref),
        (km_hbm, km_ref), (fm_hbm, fm_ref), (x_hbm, x_ref), (im_hbm, im_ref), (bdw_hbm, bdw_ref),
        (gain_hbm, gain_ref), (bias_hbm, bias_ref), (cot_hbm, cot_ref), (gamma_hbm, gamma_ref),
        (bout_hbm, bout_ref), (lm_hbm, lm_ref),
    ]
    loads = [pltpu.make_async_copy(a, b, l_sem.at[i]) for i, (a, b) in enumerate(pairs)]
    for c in loads:
        c.start()

    barrier = pltpu.get_barrier_semaphore()
    peers = [at_z(d) for d in range(1, NZ)] + [at_xc(k) for k in range(1, 2 * NX)] + [left, right]
    for dev in peers:
        pl.semaphore_signal(barrier, inc=1, device_id=dev, device_id_type=MESH)
    pl.semaphore_wait(barrier, len(peers))

    halo = launch([
        copy(x_hbm.at[pl.ds(64, 192)], halo_x.at[0], s_halo.at[0], q_halo.at[0], right),
        copy(x_hbm.at[pl.ds(0, 192)], halo_x.at[1], s_halo.at[1], q_halo.at[1], left),
    ])
    for c in loads[:3]:
        c.wait()
    row = lax.broadcasted_iota(jnp.int32, (8, 128), 0)
    col = lax.broadcasted_iota(jnp.int32, (8, 128), 1)
    wrk[...] = jnp.zeros_like(wrk)
    wrk[0:UNITS, 0:C] = win_ref[...].astype(F32)
    wrk[0:UNITS, 256:LANES] = wout_ref[:, 0:128].astype(F32)
    wrk[0:UNITS, C:256] = wout_ref[:, 128:C].astype(F32)
    wrk[UNITS : UNITS + 1, 0:UNITS] = bin_ref[...].astype(F32)
    blk_ref[...] = wrk[...].astype(BF)
    gather_a = launch([
        copy(blk_ref, wall.at[0, 0, d], s_ga.at[d - 1], q_ga.at[d - 1], at_z(d)) for d in range(1, NZ)
    ])
    wall[0, 0, 0] = blk_ref[...]
    for c in loads[3:]:
        c.wait()

    kpad[...] = jnp.zeros_like(kpad)
    for a in range(W):
        for b in range(W):
            kpad[a, 8 * b : 8 * b + W, :] = ker_ref[a, b]

    def transform(rows):
        both = dot(fm_ref[...], rows)
        return both[: 2 * NF] + both[2 * NF :]

    km = (km_ref[0], km_ref[1])

    def ker_step(a, carry):
        kf[a] = dot3(km, kpad[a])
        return carry

    lax.fori_loop(0, W, ker_step, 0)
    for p in range(SX):
        xf[3 + p] = transform(x_ref[64 * p : 64 * p + 64, :])

    arrive(gather_a)
    gather_b = launch([
        copy(wall.at[0, 0], wall.at[0, d], s_gb.at[d - 1], q_gb.at[d - 1], at_x(d)) for d in range(1, NX)
    ])

    def pass_on(d):
        return launch([copy(wall.at[0, d], wall.at[1, d], s_gc.at[d], q_gc.at[d], partner)])

    gather_c = {0: pass_on(0)}

    arrive(halo)
    has_left = (s > 0).astype(F32)
    has_right = (s < NS - 1).astype(F32)
    for p in range(3):
        xf[p] = transform(halo_x[0, 64 * p : 64 * p + 64, :]) * has_left
        xf[7 + p] = transform(halo_x[1, 64 * p : 64 * p + 64, :]) * has_right

    def forward_step(g, carry):
        top, low = pl.ds(pl.multiple_of(8 * g, 8), 8), pl.ds(pl.multiple_of(8 * g + NF, 8), 8)
        re = jnp.zeros((SX, 8, C), F32)
        im = jnp.zeros((SX, 8, C), F32)
        for a in range(W):
            kr, ki = kf[a, top, :], kf[a, low, :]
            xr, xi = xf[a : a + SX, top, :], xf[a : a + SX, low, :]
            re = re + kr * xr - ki * xi
            im = im + kr * xi + ki * xr
        yf[:, top, :] = re
        yf[:, low, :] = im
        return carry

    lax.fori_loop(0, NF // 8, forward_step, 0)
    inv = (im_ref[0], im_ref[1])
    for p in range(SX):
        mixed[64 * p : 64 * p + 64, :] = dot3(inv, yf[p]) + bdw_ref[...]

    mix = mixed[...]
    centred = mix - jnp.mean(mix, axis=-1, keepdims=True)
    inverse = lax.rsqrt(jnp.mean(centred * centred, axis=-1, keepdims=True) + 1e-06)
    unit = centred * inverse
    mixed[...] = unit
    lane = lax.broadcasted_iota(jnp.int32, (CELLS, 128), 1)
    na[:, 128:256] = jnp.where(lane == C - 128, 1.0, 0.0).astype(BF)
    na[:, 0:C] = (unit * gain_ref[...] + bias_ref[...]).astype(BF)
    d_branch = gamma_ref[...] * cot_ref[...].astype(F32)
    dba[:, 0:128] = jnp.zeros((CELLS, 128), BF)
    dba[:, 64:128] = d_branch[:, 128:C].astype(BF)
    dba[:, 128:256] = d_branch[:, 0:128].astype(BF)
    branch[...] = jnp.zeros_like(branch)
    dnorm[...] = jnp.zeros_like(dnorm)
    lane8 = lax.broadcasted_iota(jnp.int32, (2 * NZ, 8, 128), 2)
    row8 = lax.broadcasted_iota(jnp.int32, (2 * NZ, 8, 128), 1)

    def units(dc, i):
        two = pl.ds(2 * i, 2)
        block = wall[dc, two].astype(F32).reshape(2 * NZ, 8, LANES)
        t_a, t_b = block[:, :, 0:128], block[:, :, 128:256]
        tail = jnp.broadcast_to(t_a[:, UNITS : UNITS + 1, :], t_a.shape)
        b_col = jnp.sum(jnp.where(row8 == lane8, tail, 0.0), axis=2, keepdims=True)
        t_bias = jnp.where(lane8 == C - 128, b_col, t_b)
        win = jnp.concatenate([t_a.reshape(256, 128), t_bias.reshape(256, 128)], axis=1).astype(BF)
        wout = block[:, :, 128:LANES].reshape(256, 256).astype(BF)
        normed, db = na[...], dba[...]
        pre = dot_nt(normed, win)
        half_erf = 0.5 * (1.0 + lax.erf(pre * root_half))
        hidden = (pre * half_erf).astype(BF)
        slope = half_erf + pre * jnp.exp(-0.5 * pre * pre) * inv_root_tau
        branch[...] += dot(hidden, wout)
        d_pre = (dot_nt(db, wout) * slope).astype(BF)
        dnorm[...] += dot(d_pre, win)
        dwi = (dot_tn(d_pre, normed) * scale).reshape(2 * NZ, 8, 256)
        dwo = (dot_tn(hidden, db) * scale).reshape(2 * NZ, 8, 256)
        g_a, g_b = dwi[:, :, 0:128], dwi[:, :, 128:256]
        g_col = jnp.broadcast_to(g_b[:, :, C - 128 : C - 127], g_b.shape)
        g_row = jnp.sum(jnp.where(row8 == lane8, g_col, 0.0), axis=1, keepdims=True)
        g_a = jnp.where(row8 == UNITS, jnp.broadcast_to(g_row, g_a.shape), g_a)
        g_b = jnp.where(lane8 < C - 128, g_b, dwo[:, :, 0:128])
        parts = (g_a, g_b, dwo[:, :, 128:256])
        for j, part in enumerate(parts):
            part = part.reshape(2, NZ, 8, 128)
            if dc == 0:
                t1[two, :, :, 128 * j : 128 * j + 128] = part
            else:
                swall[two, :, :, 128 * j : 128 * j + 128] = part.astype(BF)

    for d in (1, 3, 2):
        arrive([gather_b[d - 1]])
        gather_c[d] = pass_on(d)
        if d == 1:
            units(0, 0)
    units(0, 1)
    scatter_c = []
    for i in range(2):
        arrive(gather_c[2 * i] + gather_c[2 * i + 1])
        units(1, i)
        two = pl.ds(2 * i, 2)
        scatter_c += launch([copy(swall.at[two], r1.at[two], s_rc.at[i], q_rc.at[i], partner)])

    cot = cot_ref[...].astype(F32)
    full = jnp.concatenate([branch[:, 128:256], branch[:, 64:128]], axis=1) + bout_ref[...]
    out_ref[...] = (x_ref[...].astype(F32) + gamma_ref[...] * full).astype(BF)
    v_gamma = jnp.sum(cot * full, axis=0, keepdims=True)
    v_bout = jnp.sum(gamma_ref[...] * cot, axis=0, keepdims=True)

    dn = dnorm[:, 0:C]
    unit2 = mixed[...]
    v_gain = jnp.sum(dn * unit2, axis=0, keepdims=True)
    v_bias = jnp.sum(dn, axis=0, keepdims=True)
    scaled = dn * gain_ref[...]
    d_mixed = inverse * (
        scaled
        - jnp.mean(scaled, axis=-1, keepdims=True)
        - unit2 * jnp.mean(scaled * unit2, axis=-1, keepdims=True)
    )
    v_bdw = jnp.sum(d_mixed, axis=0, keepdims=True)
    dmb[...] = d_mixed.astype(BF)
    halo2 = launch([
        copy(dmb.at[pl.ds(64, 192)], halo_d.at[0], s_hd.at[0], q_hd.at[0], right),
        copy(dmb.at[pl.ds(0, 192)], halo_d.at[1], s_hd.at[1], q_hd.at[1], left),
    ])
    for p in range(SX):
        df[3 + p] = transform(dmb[64 * p : 64 * p + 64, :])

    def grad_step(g, carry):
        top, low = pl.ds(pl.multiple_of(8 * g, 8), 8), pl.ds(pl.multiple_of(8 * g + NF, 8), 8)
        dr, di = df[3 : 3 + SX, top, :], df[3 : 3 + SX, low, :]
        for a in range(W):
            xr, xi = xf[a : a + SX, top, :], xf[a : a + SX, low, :]
            gf[a, top, :] = jnp.sum(dr * xr + di * xi, axis=0)
            gf[a, low, :] = jnp.sum(dr * xi - di * xr, axis=0)
        return carry

    lax.fori_loop(0, NF // 8, grad_step, 0)
    lag = (lm_ref[0], lm_ref[1])
    pay[...] = jnp.zeros_like(pay)
    vectors = [v_bdw, v_gain, v_bias, v_bout, v_gamma]
    for a in range(W):
        taps = dot3(lag, gf[a]) * scale
        for b in range(W):
            group = a * W + b
            block = taps[8 * b : 8 * b + 8, :]
            q, t = group // GROUPS, 2 * (group % GROUPS)
            pay[q, t] = block[:, 0:128]
            pay[q, t + 1, :, 0 : C - 128] = block[:, 128:C]
    for i, v in enumerate(vectors):
        pay[0, 2 * i, W : W + 1, :] = v[:, 0:128] * scale
        pay[0, 2 * i + 1, W : W + 1, 0 : C - 128] = v[:, 128:C] * scale
    payb[...] = pay[...].astype(BF)

    def chunk_of(k):
        px = lax.rem(x + k % NX, NX)
        pc = core if k < NX else 1 - core
        return pc * NX + px

    own = chunk_of(0)
    sum_x = launch([
        copy(payb.at[chunk_of(k)], rx.at[k - 1], s_px.at[k - 1], q_px.at[k - 1], at_xc(k))
        for k in range(1, 2 * NX)
    ])

    arrive(scatter_c)

    def add_core(i, carry):
        total = t1[i] + r1[i].astype(F32)
        t1[i] = total
        t1b[i] = total.astype(BF)
        return carry

    lax.fori_loop(0, NX, add_core, 0)
    scatter_b = launch([
        copy(t1b.at[d], r2.at[d - 1], s_rb.at[d - 1], q_rb.at[d - 1], at_x(-d)) for d in range(1, NX)
    ])

    arrive(halo2)
    for p in range(3):
        df[p] = transform(halo_d[0, 64 * p : 64 * p + 64, :]) * has_left
        df[7 + p] = transform(halo_d[1, 64 * p : 64 * p + 64, :]) * has_right

    arrive(sum_x)
    total = pay[own]
    for k in range(2 * NX - 1):
        total = total + rx[k].astype(F32)
    zt[...] = total
    ztb[...] = total.astype(BF)
    sum_z = launch([
        copy(ztb.at[lax.rem(z + d, NZ)], rz.at[d - 1], s_pz.at[d - 1], q_pz.at[d - 1], at_z(d))
        for d in range(1, NZ)
    ])

    def back_step(g, carry):
        top, low = pl.ds(pl.multiple_of(8 * g, 8), 8), pl.ds(pl.multiple_of(8 * g + NF, 8), 8)
        re = jnp.zeros((SX, 8, C), F32)
        im = jnp.zeros((SX, 8, C), F32)
        for a in range(W):
            kr, ki = kf[W - 1 - a, top, :], kf[W - 1 - a, low, :]
            dr, di = df[a : a + SX, top, :], df[a : a + SX, low, :]
            re = re + kr * dr + ki * di
            im = im + kr * di - ki * dr
        yf[:, top, :] = re
        yf[:, low, :] = im
        return carry

    lax.fori_loop(0, NF // 8, back_step, 0)

    arrive(scatter_b)
    t2v = t1[0]
    for d in range(NX - 1):
        t2v = t2v + r2[d].astype(F32)
    t2[...] = t2v
    t2b[...] = t2v.astype(BF)
    scatter_a = launch([
        copy(t2b.at[d], r3.at[d - 1], s_ra.at[d - 1], q_ra.at[d - 1], at_z(-d)) for d in range(1, NZ)
    ])

    arrive(sum_z)
    tile = zt[z]
    for d in range(NZ - 1):
        tile = tile + rz[d].astype(F32)
    agz[z] = tile.astype(BF)
    gather_z = launch([
        copy(agz.at[z], agz.at[z], s_az.at[d - 1], q_az.at[d - 1], at_z(d)) for d in range(1, NZ)
    ])

    for p in range(SX):
        rows = slice(64 * p, 64 * p + 64)
        dx_ref[rows, :] = (cot_ref[rows, :].astype(F32) + dot3(inv, yf[p])).astype(BF)

    arrive(gather_z)
    fin[own] = agz[...]
    gather_x = launch([
        copy(agz, fin.at[own], s_ax.at[k - 1], q_ax.at[k - 1], at_xc(k)) for k in range(1, 2 * NX)
    ])

    arrive(scatter_a)
    mine = t2[0]
    for d in range(NZ - 1):
        mine = mine + r3[d].astype(F32)
    dwi_ref[...] = mine[0:UNITS, 0:C]
    dwo_ref[:, 0:128] = mine[0:UNITS, 256:LANES]
    dwo_ref[:, 128:C] = mine[0:UNITS, C:256]
    dbi_ref[...] = mine[UNITS : UNITS + 1, 0:UNITS]

    arrive(gather_x)
    for group in range(W * W):
        q, t = group // GROUPS, 2 * (group % GROUPS)
        first, second = fin[q, t].astype(F32), fin[q, t + 1].astype(F32)
        dker_ref[group // W, group % W, :, 0:128] = first[0:W]
        dker_ref[group // W, group % W, :, 128:C] = second[0:W, 0 : C - 128]
        if group < 5:
            v_ref = (vbdw_ref, vgain_ref, vbias_ref, vbout_ref, vgamma_ref)[group]
            v_ref[:, 0:128] = first[W : W + 1]
            v_ref[:, 128:C] = second[W : W + 1, 0 : C - 128]

    for c in pending:
        c.wait_send()


def emit_body(*refs):
    n = (len(refs) - 1) // 2
    sems = refs[-1]
    copies = [pltpu.make_async_copy(refs[i], refs[n + i], sems.at[i]) for i in range(n)]
    for c in copies:
        c.start()
    for c in copies:
        c.wait()


def on_device(
    features, cotangent, kernel, b_dw, ln_gain, ln_bias, w_in_t, b_in, w_out, b_out, gamma
):
    operands = [
        features.reshape(CELLS, C), cotangent.reshape(CELLS, C), kernel,
        b_dw.reshape(1, C), ln_gain.reshape(1, C), ln_bias.reshape(1, C), w_in_t,
        b_in.reshape(1, UNITS), w_out, b_out.reshape(1, C), gamma.reshape(1, C),
    ] + [jnp.asarray(m) for m in transforms()]
    vm = pl.BlockSpec(memory_space=pltpu.VMEM)
    hbm = pl.BlockSpec(memory_space=pltpu.HBM)
    dma = pltpu.SemaphoreType.DMA
    counts = [2, NZ - 1, NX - 1, NX, 2, 2, NX - 1, NZ - 1, 2 * NX - 1, NZ - 1, NZ - 1, 2 * NX - 1]
    sems = [dma((n,)) for n in counts for _ in range(2)]
    scratch = [pltpu.VMEM(o.shape, o.dtype) for o in operands] + [
        dma((len(operands),)),
        pltpu.VMEM((8, LANES), BF),
        pltpu.VMEM((2, 192, C), BF),
        pltpu.VMEM((2, 192, C), BF),
        pltpu.VMEM((2, NX, NZ, 8, LANES), BF),
        pltpu.VMEM((NX, NZ, 8, LANES), BF),
        pltpu.VMEM((NX, NZ, 8, LANES), BF),
        pltpu.VMEM((NX, NZ, 8, LANES), F32),
        pltpu.VMEM((NX, NZ, 8, LANES), BF),
        pltpu.VMEM((NX - 1, NZ, 8, LANES), BF),
        pltpu.VMEM((NZ, 8, LANES), F32),
        pltpu.VMEM((NZ, 8, LANES), BF),
        pltpu.VMEM((NZ - 1, 8, LANES), BF),
        pltpu.VMEM((W, 8 * W, C), F32),
        pltpu.VMEM((W, 2 * NF, C), F32),
        pltpu.VMEM((SX + 6, 2 * NF, C), F32),
        pltpu.VMEM((SX + 6, 2 * NF, C), F32),
        pltpu.VMEM((SX, 2 * NF, C), F32),
        pltpu.VMEM((W, 2 * NF, C), F32),
        pltpu.VMEM((CELLS, C), F32),
        pltpu.VMEM((CELLS, 256), BF),
        pltpu.VMEM((CELLS, 256), BF),
        pltpu.VMEM((CELLS, 256), F32),
        pltpu.VMEM((CELLS, 256), F32),
        pltpu.VMEM((CELLS, C), BF),
        pltpu.VMEM((2 * NX, NZ, 8, 128), F32),
        pltpu.VMEM((2 * NX, NZ, 8, 128), BF),
        pltpu.VMEM((2 * NX - 1, NZ, 8, 128), BF),
        pltpu.VMEM((NZ, 8, 128), F32),
        pltpu.VMEM((NZ, 8, 128), BF),
        pltpu.VMEM((NZ - 1, 8, 128), BF),
        pltpu.VMEM((NZ, 8, 128), BF),
        pltpu.VMEM((2 * NX, NZ, 8, 128), BF),
        pltpu.VMEM((8, LANES), F32),
    ]
    vec = jax.ShapeDtypeStruct((1, C), F32)
    shapes = (
        jax.ShapeDtypeStruct((CELLS, C), BF),
        jax.ShapeDtypeStruct((CELLS, C), BF),
        jax.ShapeDtypeStruct((W, W, W, C), F32),
        vec, vec, vec,
        jax.ShapeDtypeStruct((UNITS, C), F32),
        jax.ShapeDtypeStruct((1, UNITS), F32),
        jax.ShapeDtypeStruct((UNITS, C), F32),
        vec, vec,
    )
    results = pl.pallas_call(
        kernel_body,
        out_shape=shapes,
        in_specs=[hbm] * len(operands),
        out_specs=(vm,) * len(shapes),
        scratch_shapes=scratch + sems,
        compiler_params=pltpu.CompilerParams(
            collective_id=0, has_side_effects=True, vmem_limit_bytes=48 * 1024 * 1024
        ),
    )(*[pltpu.with_memory_space_constraint(o, pltpu.HBM) for o in operands])
    results = pl.pallas_call(
        emit_body,
        out_shape=shapes,
        in_specs=[vm] * len(shapes),
        out_specs=(hbm,) * len(shapes),
        scratch_shapes=[dma((len(shapes),))],
    )(*[pltpu.with_memory_space_constraint(o, pltpu.VMEM) for o in results])
    out, dx, dker, bdw, gain, bias, dwi, dbi, dwo, bout, gam = results
    return (
        out.reshape(features.shape), dx.reshape(features.shape), dker,
        bdw.reshape(C), gain.reshape(C), bias.reshape(C), dwi, dbi.reshape(UNITS), dwo,
        bout.reshape(C), gam.reshape(C),
    )


def solution(mesh):
    cells = P(("crop", "space"), None, None, None)
    rows = P(("crop", "space"), None)
    in_specs = (
        cells, cells, P(), P(), P(), P(), P("space", None), P("space"), P("space", None), P(), P(),
    )
    out_specs = (
        cells, cells, P("crop", None, None, None), P("crop"), P("crop"), P("crop"),
        rows, P(("crop", "space")), rows, P("crop"), P("crop"),
    )
    return jax.shard_map(
        on_device, mesh=mesh, in_specs=in_specs, out_specs=out_specs, check_vma=False
    )
```

```python
import numpy as np
import jax
import jax.numpy as jnp
import ml_dtypes
from jax import lax
from jax.experimental import pallas as pl
from jax.experimental.pallas import tpu as pltpu
from jax.sharding import PartitionSpec as P

root_half = 0.7071067811865476
inv_root_tau = 0.3989422804014327
MESH = pl.DeviceIdType.MESH
F32 = jnp.float32
BF = jnp.bfloat16

NX, NZ, NS = 4, 16, 128
C = 192
W = 7
G = 8
SX = 4
CELLS = SX * G * G
N = 11
NF = 64
UNITS = 6
LANES = 384
CHUNK = 10
ORDER = (0, 1, 15, 2, 14, 3, 13, 4, 12, 5, 11, 6, 10, 7, 9, 8)
BANDS = ((0, 6), (6, 11), (11, 16))


def split_np(m):
    high = m.astype(ml_dtypes.bfloat16)
    low = (m - high.astype(np.float64)).astype(ml_dtypes.bfloat16)
    return high, low


def transforms():
    seen, reps = set(), []
    for u in range(N):
        for v in range(N):
            if (u, v) in seen:
                continue
            reps.append((u, v))
            seen.add((u, v))
            seen.add(((-u) % N, (-v) % N))
    u = np.array([r[0] for r in reps])[:, None]
    v = np.array([r[1] for r in reps])[:, None]
    weight = np.where((u == 0) & (v == 0), 1.0, 2.0) / N**2
    n = len(reps)

    def table(pos_j, pos_k, live, sign):
        angle = 2 * np.pi / N * (u * pos_j[None] + v * pos_k[None])
        out = np.zeros((2 * NF, len(pos_j)))
        out[:n] = np.cos(angle) * live
        out[NF : NF + n] = sign * np.sin(angle) * live
        return out

    scale = np.zeros((2 * NF, 1))
    scale[:n] = weight
    scale[NF : NF + n] = weight
    cell = np.arange(G * G)
    tap = np.arange(8 * W)
    live = ((tap % 8) < W)[None]
    fwd = table(cell // G, cell % G, 1.0, -1.0)
    inv = (fwd * scale).T
    ker = table(tap // 8 - 3, tap % 8 - 3, live, 1.0)
    lag = (table(tap // 8 - 3, tap % 8 - 3, live, -1.0) * scale).T
    fm = np.concatenate(split_np(fwd), axis=0)
    return fm, np.stack(split_np(ker)), np.stack(split_np(inv)), np.stack(split_np(lag))


def dot(a, b):
    return jnp.dot(a, b, preferred_element_type=F32)


def dot_nt(a, b):
    return lax.dot_general(a, b, (((1,), (1,)), ((), ())), preferred_element_type=F32)


def dot_tn(a, b):
    return lax.dot_general(a, b, (((0,), (0,)), ((), ())), preferred_element_type=F32)


def halves(value):
    high = value.astype(BF)
    return high, (value - high.astype(F32)).astype(BF)


def dot3(m, value):
    high, low = halves(value)
    return dot(m[0], high) + dot(m[1], high) + dot(m[0], low)


def kernel_body(
    x_hbm, cot_hbm, ker_hbm, bdw_hbm, gain_hbm, bias_hbm, win_hbm, bin_hbm, wout_hbm, bout_hbm,
    gamma_hbm, fm_hbm, km_hbm, im_hbm, lm_hbm,
    out_ref, dx_ref, dker_ref, vbdw_ref, vgain_ref, vbias_ref, dwi_ref, dbi_ref, dwo_ref,
    vbout_ref, vgamma_ref,
    x_ref, cot_ref, ker_ref, bdw_ref, gain_ref, bias_ref, win_ref, bin_ref, wout_ref, bout_ref,
    gamma_ref, fm_ref, km_ref, im_ref, lm_ref, l_sem, blk_ref,
    halo_x, halo_d, wall, swall, r1, t1, t1b, r2, t2, t2b, r3,
    kpad, kf, xf, df, yf, gf, mixed, na, dba, branch, dnorm, dmb,
    pay, payb, rx, zt, ztb, rz, agz, fin, wrk, hid, dpb,
    s_halo, q_halo, s_ga, q_ga, s_gb, q_gb, s_gc, q_gc, s_hd, q_hd,
    s_rc, q_rc, s_rb, q_rb, s_ra, q_ra, s_px, q_px, s_pz, q_pz, s_az, q_az, s_ax, q_ax,
):
    scale = float(NS * CELLS) ** (-0.5)
    s = lax.axis_index("space")
    core = lax.rem(s, 2)
    z = lax.rem(s // 2, NZ)
    x = s // (2 * NZ)

    def place(px, pz, pc):
        return {"space": (px * NZ + pz) * 2 + pc}

    def at_z(d):
        return place(x, lax.rem(z + d + NZ, NZ), core)

    def at_x(d):
        return place(lax.rem(x + d + NX, NX), z, core)

    def at_xc(k):
        return place(lax.rem(x + k % NX, NX), z, core if k < NX else 1 - core)

    partner = place(x, z, 1 - core)
    right = {"space": lax.rem(s + 1, NS)}
    left = {"space": lax.rem(s + NS - 1, NS)}

    def copy(src, dst, ssem, rsem, dev):
        return pltpu.make_async_remote_copy(
            src_ref=src, dst_ref=dst, send_sem=ssem, recv_sem=rsem, device_id=dev, device_id_type=MESH
        )

    pending = []

    def launch(copies):
        for c in copies:
            c.start()
        pending.extend(copies)
        return copies

    def arrive(copies):
        for c in copies:
            c.wait_recv()

    pairs = [
        (win_hbm, win_ref), (bin_hbm, bin_ref), (wout_hbm, wout_ref), (ker_hbm, ker_ref),
        (km_hbm, km_ref), (fm_hbm, fm_ref), (x_hbm, x_ref), (im_hbm, im_ref), (bdw_hbm, bdw_ref),
        (gain_hbm, gain_ref), (bias_hbm, bias_ref), (cot_hbm, cot_ref), (gamma_hbm, gamma_ref),
        (bout_hbm, bout_ref), (lm_hbm, lm_ref),
    ]
    loads = [pltpu.make_async_copy(a, b, l_sem.at[i]) for i, (a, b) in enumerate(pairs)]
    for c in loads:
        c.start()

    barrier = pltpu.get_barrier_semaphore()
    peers = [at_z(d) for d in range(1, NZ)] + [at_xc(k) for k in range(1, 2 * NX)] + [left, right]
    for dev in peers:
        pl.semaphore_signal(barrier, inc=1, device_id=dev, device_id_type=MESH)
    pl.semaphore_wait(barrier, len(peers))

    for c in loads[:3]:
        c.wait()
    row = lax.broadcasted_iota(jnp.int32, (8, 128), 0)
    col = lax.broadcasted_iota(jnp.int32, (8, 128), 1)
    wrk[...] = jnp.zeros_like(wrk)
    wrk[0:UNITS, 0:C] = win_ref[...].astype(F32)
    wrk[0:UNITS, 256:LANES] = wout_ref[:, 0:128].astype(F32)
    wrk[0:UNITS, C:256] = wout_ref[:, 128:C].astype(F32)
    wrk[UNITS : UNITS + 1, 0:UNITS] = bin_ref[...].astype(F32)
    blk_ref[...] = wrk[...].astype(BF)
    gather_a = launch([
        copy(blk_ref, wall.at[0, 0, i], s_ga.at[i - 1], q_ga.at[i - 1], at_z(ORDER[i]))
        for i in range(NZ - 1, 0, -1)
    ])[::-1]
    halo = launch([
        copy(x_hbm.at[pl.ds(64, 192)], halo_x.at[0], s_halo.at[0], q_halo.at[0], right),
        copy(x_hbm.at[pl.ds(0, 192)], halo_x.at[1], s_halo.at[1], q_halo.at[1], left),
    ])
    wall[0, 0, 0] = blk_ref[...]
    for c in loads[3:]:
        c.wait()

    kpad[...] = jnp.zeros_like(kpad)
    for a in range(W):
        for b in range(W):
            kpad[a, 8 * b : 8 * b + W, :] = ker_ref[a, b]

    def transform(rows):
        both = dot(fm_ref[...], rows)
        return both[: 2 * NF] + both[2 * NF :]

    km = (km_ref[0], km_ref[1])

    def ker_step(a, carry):
        kf[a] = dot3(km, kpad[a])
        return carry

    lax.fori_loop(0, W, ker_step, 0)
    for p in range(SX):
        xf[3 + p] = transform(x_ref[64 * p : 64 * p + 64, :])

    arrive(halo)
    has_left = (s > 0).astype(F32)
    has_right = (s < NS - 1).astype(F32)
    for p in range(3):
        xf[p] = transform(halo_x[0, 64 * p : 64 * p + 64, :]) * has_left
        xf[7 + p] = transform(halo_x[1, 64 * p : 64 * p + 64, :]) * has_right

    def forward_step(g, carry):
        top, low = pl.ds(pl.multiple_of(8 * g, 8), 8), pl.ds(pl.multiple_of(8 * g + NF, 8), 8)
        re = jnp.zeros((SX, 8, C), F32)
        im = jnp.zeros((SX, 8, C), F32)
        for a in range(W):
            kr, ki = kf[a, top, :], kf[a, low, :]
            xr, xi = xf[a : a + SX, top, :], xf[a : a + SX, low, :]
            re = re + kr * xr - ki * xi
            im = im + kr * xi + ki * xr
        yf[:, top, :] = re
        yf[:, low, :] = im
        return carry

    lax.fori_loop(0, NF // 8, forward_step, 0)
    inv = (im_ref[0], im_ref[1])
    for p in range(SX):
        mixed[64 * p : 64 * p + 64, :] = dot3(inv, yf[p]) + bdw_ref[...]

    mix = mixed[...]
    centred = mix - jnp.mean(mix, axis=-1, keepdims=True)
    inverse = lax.rsqrt(jnp.mean(centred * centred, axis=-1, keepdims=True) + 1e-06)
    unit = centred * inverse
    mixed[...] = unit
    lane = lax.broadcasted_iota(jnp.int32, (CELLS, 128), 1)
    na[:, 128:256] = jnp.where(lane == C - 128, 1.0, 0.0).astype(BF)
    na[:, 0:C] = (unit * gain_ref[...] + bias_ref[...]).astype(BF)
    d_branch = gamma_ref[...] * cot_ref[...].astype(F32)
    dba[:, 0:128] = jnp.zeros((CELLS, 128), BF)
    dba[:, 64:128] = d_branch[:, 128:C].astype(BF)
    dba[:, 128:256] = d_branch[:, 0:128].astype(BF)
    branch[...] = jnp.zeros_like(branch)
    dnorm[...] = jnp.zeros_like(dnorm)
    lane8 = lax.broadcasted_iota(jnp.int32, (2 * NZ, 8, 128), 2)
    row8 = lax.broadcasted_iota(jnp.int32, (2 * NZ, 8, 128), 1)

    gather_b, gather_c = {}, {}

    def band(dc, d, k):
        lo, hi = BANDS[k]
        return wall.at[dc, d, pl.ds(lo, hi - lo)]

    def pass_on(d, k):
        i = 3 * d + k
        gather_c[d, k] = launch([
            copy(band(0, d, k), band(1, d, k), s_gc.at[i], q_gc.at[i], partner)
        ])

    for k in range(3):
        lo, hi = BANDS[k]
        arrive(gather_a[max(lo, 1) - 1 : hi - 1])
        for d in (2, 1, 3):
            i = 3 * (d - 1) + k
            gather_b[d, k] = launch([
                copy(band(0, 0, k), band(0, d, k), s_gb.at[i], q_gb.at[i], at_x(d))
            ])
        pass_on(0, k)

    def units(dc, i):
        two = pl.ds(2 * i, 2)
        block = wall[dc, two].astype(F32).reshape(2 * NZ, 8, LANES)
        t_a, t_b = block[:, :, 0:128], block[:, :, 128:256]
        tail = jnp.broadcast_to(t_a[:, UNITS : UNITS + 1, :], t_a.shape)
        b_col = jnp.sum(jnp.where(row8 == lane8, tail, 0.0), axis=2, keepdims=True)
        t_bias = jnp.where(lane8 == C - 128, b_col, t_b)
        win = jnp.concatenate([t_a.reshape(256, 128), t_bias.reshape(256, 128)], axis=1).astype(BF)
        wout = block[:, :, 128:LANES].reshape(256, 256).astype(BF)
        normed, db = na[...], dba[...]
        pre = dot_nt(normed, win)
        half_erf = 0.5 * (1.0 + lax.erf(pre * root_half))
        hidden = (pre * half_erf).astype(BF)
        hid[dc, i] = hidden
        slope = half_erf + pre * jnp.exp(-0.5 * pre * pre) * inv_root_tau
        branch[...] += dot(hidden, wout)
        d_pre = (dot_nt(db, wout) * slope).astype(BF)
        dpb[dc, i] = d_pre
        dnorm[...] += dot(d_pre, win)

    def gradients(dc, i):
        two = pl.ds(2 * i, 2)
        hidden, d_pre, normed, db = hid[dc, i], dpb[dc, i], na[...], dba[...]
        dwi = (dot_tn(d_pre, normed) * scale).reshape(2 * NZ, 8, 256)
        dwo = (dot_tn(hidden, db) * scale).reshape(2 * NZ, 8, 256)
        g_a, g_b = dwi[:, :, 0:128], dwi[:, :, 128:256]
        g_col = jnp.broadcast_to(g_b[:, :, C - 128 : C - 127], g_b.shape)
        g_row = jnp.sum(jnp.where(row8 == lane8, g_col, 0.0), axis=1, keepdims=True)
        g_a = jnp.where(row8 == UNITS, jnp.broadcast_to(g_row, g_a.shape), g_a)
        g_b = jnp.where(lane8 < C - 128, g_b, dwo[:, :, 0:128])
        parts = (g_a, g_b, dwo[:, :, 128:256])
        for j, part in enumerate(parts):
            part = part.reshape(2, NZ, 8, 128)
            if dc == 0:
                t1[two, :, :, 128 * j : 128 * j + 128] = part
            else:
                swall[two, :, :, 128 * j : 128 * j + 128] = part.astype(BF)

    for k in range(3):
        for d in (1, 3, 2):
            arrive(gather_b[d, k])
            pass_on(d, k)
    for i in range(2):
        units(0, i)
    for i in range(2):
        for d in (2 * i, 2 * i + 1):
            for k in range(3):
                arrive(gather_c[d, k])
        units(1, i)

    cot = cot_ref[...].astype(F32)
    full = jnp.concatenate([branch[:, 128:256], branch[:, 64:128]], axis=1) + bout_ref[...]
    v_gamma = jnp.sum(cot * full, axis=0, keepdims=True)
    v_bout = jnp.sum(gamma_ref[...] * cot, axis=0, keepdims=True)

    dn = dnorm[:, 0:C]
    unit2 = mixed[...]
    v_gain = jnp.sum(dn * unit2, axis=0, keepdims=True)
    v_bias = jnp.sum(dn, axis=0, keepdims=True)
    scaled = dn * gain_ref[...]
    d_mixed = inverse * (
        scaled
        - jnp.mean(scaled, axis=-1, keepdims=True)
        - unit2 * jnp.mean(scaled * unit2, axis=-1, keepdims=True)
    )
    v_bdw = jnp.sum(d_mixed, axis=0, keepdims=True)
    dmb[...] = d_mixed.astype(BF)
    halo2 = launch([
        copy(dmb.at[pl.ds(64, 192)], halo_d.at[0], s_hd.at[0], q_hd.at[0], right),
        copy(dmb.at[pl.ds(0, 192)], halo_d.at[1], s_hd.at[1], q_hd.at[1], left),
    ])
    for p in range(SX):
        df[3 + p] = transform(dmb[64 * p : 64 * p + 64, :])

    def grad_step(g, carry):
        top, low = pl.ds(pl.multiple_of(8 * g, 8), 8), pl.ds(pl.multiple_of(8 * g + NF, 8), 8)
        dr, di = df[3 : 3 + SX, top, :], df[3 : 3 + SX, low, :]
        for a in range(W):
            xr, xi = xf[a : a + SX, top, :], xf[a : a + SX, low, :]
            gf[a, top, :] = jnp.sum(dr * xr + di * xi, axis=0)
            gf[a, low, :] = jnp.sum(dr * xi - di * xr, axis=0)
        return carry

    lax.fori_loop(0, NF // 8, grad_step, 0)
    lag = (lm_ref[0], lm_ref[1])
    pay[...] = jnp.zeros_like(pay)
    vectors = [v_bdw, v_gain, v_bias, v_bout, v_gamma]
    for a in range(W):
        taps = dot3(lag, gf[a]) * scale
        for b in range(W):
            group = a * W + b
            block = taps[8 * b : 8 * b + 8, :]
            q, t, r, u, at = spot(group)
            pay[q, t] = block[:, 0:128]
            pay[r, u, :, at : at + C - 128] = block[:, 128:C]
    for i, v in enumerate(vectors):
        q, t, r, u, at = spot(i)
        pay[q, t, W : W + 1, :] = v[:, 0:128] * scale
        pay[r, u, W : W + 1, at : at + C - 128] = v[:, 128:C] * scale
    payb[...] = pay[...].astype(BF)
    zt[pl.ds(CHUNK, NZ - CHUNK)] = jnp.zeros((NZ - CHUNK, 8, 128), F32)
    ztb[pl.ds(CHUNK, NZ - CHUNK)] = jnp.zeros((NZ - CHUNK, 8, 128), BF)

    def chunk_of(k):
        px = lax.rem(x + k % NX, NX)
        pc = core if k < NX else 1 - core
        return pc * NX + px

    own = chunk_of(0)
    sum_x = launch([
        copy(payb.at[chunk_of(k)], rx.at[k - 1], s_px.at[k - 1], q_px.at[k - 1], at_xc(k))
        for k in range(1, 2 * NX)
    ])

    scatter_c = []
    for i in range(2):
        gradients(1, i)
        two = pl.ds(2 * i, 2)
        scatter_c += launch([copy(swall.at[two], r1.at[two], s_rc.at[i], q_rc.at[i], partner)])
    arrive(halo2)
    for p in range(3):
        df[p] = transform(halo_d[0, 64 * p : 64 * p + 64, :]) * has_left
        df[7 + p] = transform(halo_d[1, 64 * p : 64 * p + 64, :]) * has_right
    for i in range(2):
        gradients(0, i)
    arrive(scatter_c)

    def add_core(i, carry):
        total = t1[i] + r1[i].astype(F32)
        t1[i] = total
        t1b[i] = total.astype(BF)
        return carry

    lax.fori_loop(0, NX, add_core, 0)
    scatter_b = launch([
        copy(t1b.at[d], r2.at[d - 1], s_rb.at[d - 1], q_rb.at[d - 1], at_x(-d)) for d in range(1, NX)
    ])

    arrive(sum_x)
    total = pay[own]
    for k in range(2 * NX - 1):
        total = total + rx[k].astype(F32)
    zt[pl.ds(0, CHUNK)] = total
    ztb[pl.ds(0, CHUNK)] = total.astype(BF)
    sum_z = launch([
        copy(
            ztb.at[lax.rem(z + ORDER[i], NZ)], rz.at[i - 1], s_pz.at[i - 1], q_pz.at[i - 1],
            at_z(ORDER[i]),
        )
        for i in range(NZ - 1, 0, -1)
    ])

    def back_step(g, carry):
        top, low = pl.ds(pl.multiple_of(8 * g, 8), 8), pl.ds(pl.multiple_of(8 * g + NF, 8), 8)
        re = jnp.zeros((SX, 8, C), F32)
        im = jnp.zeros((SX, 8, C), F32)
        for a in range(W):
            kr, ki = kf[W - 1 - a, top, :], kf[W - 1 - a, low, :]
            dr, di = df[a : a + SX, top, :], df[a : a + SX, low, :]
            re = re + kr * dr + ki * di
            im = im + kr * di - ki * dr
        yf[:, top, :] = re
        yf[:, low, :] = im
        return carry

    lax.fori_loop(0, NF // 8, back_step, 0)

    arrive(scatter_b)
    t2v = t1[0]
    for d in range(NX - 1):
        t2v = t2v + r2[d].astype(F32)
    t2[...] = t2v
    t2b[...] = t2v.astype(BF)
    scatter_a = launch([
        copy(t2b.at[i], r3.at[i - 1], s_ra.at[i - 1], q_ra.at[i - 1], at_z(-ORDER[i]))
        for i in range(NZ - 1, 0, -1)
    ])

    arrive(sum_z)
    tile = zt[z]
    for i in range(NZ - 1):
        tile = tile + rz[i].astype(F32)
    agz[z] = tile.astype(BF)
    gather_z = launch([
        copy(agz.at[z], agz.at[z], s_az.at[i - 1], q_az.at[i - 1], at_z(ORDER[i]))
        for i in range(NZ - 1, 0, -1)
    ])

    full = jnp.concatenate([branch[:, 128:256], branch[:, 64:128]], axis=1) + bout_ref[...]
    out_ref[...] = (x_ref[...].astype(F32) + gamma_ref[...] * full).astype(BF)
    for p in range(SX):
        rows = slice(64 * p, 64 * p + 64)
        dx_ref[rows, :] = (cot_ref[rows, :].astype(F32) + dot3(inv, yf[p])).astype(BF)

    arrive(gather_z)
    fin[own] = agz[pl.ds(0, CHUNK)]
    gather_x = launch([
        copy(agz.at[pl.ds(0, CHUNK)], fin.at[own], s_ax.at[k - 1], q_ax.at[k - 1], at_xc(k)) for k in range(1, 2 * NX)
    ])

    arrive(scatter_a)
    mine = t2[0]
    for d in range(NZ - 1):
        mine = mine + r3[d].astype(F32)
    dwi_ref[...] = mine[0:UNITS, 0:C]
    dwo_ref[:, 0:128] = mine[0:UNITS, 256:LANES]
    dwo_ref[:, 128:C] = mine[0:UNITS, C:256]
    dbi_ref[...] = mine[UNITS : UNITS + 1, 0:UNITS]

    arrive(gather_x)
    for group in range(W * W):
        q, t, r, u, at = spot(group)
        first, second = fin[q, t].astype(F32), fin[r, u].astype(F32)[:, at : at + C - 128]
        dker_ref[group // W, group % W, :, 0:128] = first[0:W]
        dker_ref[group // W, group % W, :, 128:C] = second[0:W]
        if group < 5:
            v_ref = (vbdw_ref, vgain_ref, vbias_ref, vbout_ref, vgamma_ref)[group]
            v_ref[:, 0:128] = first[W : W + 1]
            v_ref[:, 128:C] = second[W : W + 1]

    for c in pending:
        c.wait_send()


def spot(group):
    first = 3 * (group // 2)
    whole, part = first + group % 2, first + 2
    return whole // CHUNK, whole % CHUNK, part // CHUNK, part % CHUNK, (C - 128) * (group % 2)


def emit_body(*refs):
    n = (len(refs) - 1) // 2
    sems = refs[-1]
    copies = [pltpu.make_async_copy(refs[i], refs[n + i], sems.at[i]) for i in range(n)]
    for c in copies:
        c.start()
    for c in copies:
        c.wait()


def on_device(
    features, cotangent, kernel, b_dw, ln_gain, ln_bias, w_in_t, b_in, w_out, b_out, gamma
):
    operands = [
        features.reshape(CELLS, C), cotangent.reshape(CELLS, C), kernel,
        b_dw.reshape(1, C), ln_gain.reshape(1, C), ln_bias.reshape(1, C), w_in_t,
        b_in.reshape(1, UNITS), w_out, b_out.reshape(1, C), gamma.reshape(1, C),
    ] + [jnp.asarray(m) for m in transforms()]
    vm = pl.BlockSpec(memory_space=pltpu.VMEM)
    hbm = pl.BlockSpec(memory_space=pltpu.HBM)
    dma = pltpu.SemaphoreType.DMA
    counts = [2, NZ - 1, 9, 12, 2, 2, NX - 1, NZ - 1, 2 * NX - 1, NZ - 1, NZ - 1, 2 * NX - 1]
    sems = [dma((n,)) for n in counts for _ in range(2)]
    scratch = [pltpu.VMEM(o.shape, o.dtype) for o in operands] + [
        dma((len(operands),)),
        pltpu.VMEM((8, LANES), BF),
        pltpu.VMEM((2, 192, C), BF),
        pltpu.VMEM((2, 192, C), BF),
        pltpu.VMEM((2, NX, NZ, 8, LANES), BF),
        pltpu.VMEM((NX, NZ, 8, LANES), BF),
        pltpu.VMEM((NX, NZ, 8, LANES), BF),
        pltpu.VMEM((NX, NZ, 8, LANES), F32),
        pltpu.VMEM((NX, NZ, 8, LANES), BF),
        pltpu.VMEM((NX - 1, NZ, 8, LANES), BF),
        pltpu.VMEM((NZ, 8, LANES), F32),
        pltpu.VMEM((NZ, 8, LANES), BF),
        pltpu.VMEM((NZ - 1, 8, LANES), BF),
        pltpu.VMEM((W, 8 * W, C), F32),
        pltpu.VMEM((W, 2 * NF, C), F32),
        pltpu.VMEM((SX + 6, 2 * NF, C), F32),
        pltpu.VMEM((SX + 6, 2 * NF, C), F32),
        pltpu.VMEM((SX, 2 * NF, C), F32),
        pltpu.VMEM((W, 2 * NF, C), F32),
        pltpu.VMEM((CELLS, C), F32),
        pltpu.VMEM((CELLS, 256), BF),
        pltpu.VMEM((CELLS, 256), BF),
        pltpu.VMEM((CELLS, 256), F32),
        pltpu.VMEM((CELLS, 256), F32),
        pltpu.VMEM((CELLS, C), BF),
        pltpu.VMEM((2 * NX, CHUNK, 8, 128), F32),
        pltpu.VMEM((2 * NX, CHUNK, 8, 128), BF),
        pltpu.VMEM((2 * NX - 1, CHUNK, 8, 128), BF),
        pltpu.VMEM((NZ, 8, 128), F32),
        pltpu.VMEM((NZ, 8, 128), BF),
        pltpu.VMEM((NZ - 1, 8, 128), BF),
        pltpu.VMEM((NZ, 8, 128), BF),
        pltpu.VMEM((2 * NX, CHUNK, 8, 128), BF),
        pltpu.VMEM((8, LANES), F32),
        pltpu.VMEM((2, 2, CELLS, 256), BF),
        pltpu.VMEM((2, 2, CELLS, 256), BF),
    ]
    vec = jax.ShapeDtypeStruct((1, C), F32)
    shapes = (
        jax.ShapeDtypeStruct((CELLS, C), BF),
        jax.ShapeDtypeStruct((CELLS, C), BF),
        jax.ShapeDtypeStruct((W, W, W, C), F32),
        vec, vec, vec,
        jax.ShapeDtypeStruct((UNITS, C), F32),
        jax.ShapeDtypeStruct((1, UNITS), F32),
        jax.ShapeDtypeStruct((UNITS, C), F32),
        vec, vec,
    )
    results = pl.pallas_call(
        kernel_body,
        out_shape=shapes,
        in_specs=[hbm] * len(operands),
        out_specs=(vm,) * len(shapes),
        scratch_shapes=scratch + sems,
        compiler_params=pltpu.CompilerParams(
            collective_id=0, has_side_effects=True, vmem_limit_bytes=48 * 1024 * 1024
        ),
    )(*[pltpu.with_memory_space_constraint(o, pltpu.HBM) for o in operands])
    results = pl.pallas_call(
        emit_body,
        out_shape=shapes,
        in_specs=[vm] * len(shapes),
        out_specs=(hbm,) * len(shapes),
        scratch_shapes=[dma((len(shapes),))],
    )(*[pltpu.with_memory_space_constraint(o, pltpu.VMEM) for o in results])
    out, dx, dker, bdw, gain, bias, dwi, dbi, dwo, bout, gam = results
    return (
        out.reshape(features.shape), dx.reshape(features.shape), dker,
        bdw.reshape(C), gain.reshape(C), bias.reshape(C), dwi, dbi.reshape(UNITS), dwo,
        bout.reshape(C), gam.reshape(C),
    )


def solution(mesh):
    cells = P(("crop", "space"), None, None, None)
    rows = P(("crop", "space"), None)
    in_specs = (
        cells, cells, P(), P(), P(), P(), P("space", None), P("space"), P("space", None), P(), P(),
    )
    out_specs = (
        cells, cells, P("crop", None, None, None), P("crop"), P("crop"), P("crop"),
        rows, P(("crop", "space")), rows, P("crop"), P("crop"),
    )
    return jax.shard_map(
        on_device, mesh=mesh, in_specs=in_specs, out_specs=out_specs, check_vma=False
    )
```

```python
import numpy as np
import jax
import jax.numpy as jnp
import ml_dtypes
from jax import lax
from jax.experimental import pallas as pl
from jax.experimental.pallas import tpu as pltpu
from jax.sharding import PartitionSpec as P

root_half = 0.7071067811865476
inv_root_tau = 0.3989422804014327
MESH = pl.DeviceIdType.MESH
F32 = jnp.float32
BF = jnp.bfloat16

NX, NZ, NS = 4, 16, 128
C = 192
W = 7
G = 8
SX = 4
CELLS = SX * G * G
N = 11
NF = 64
UNITS = 6
LANES = 384
CHUNK = 10
ORDER = (0, 1, 15, 2, 14, 3, 13, 4, 12, 5, 11, 6, 10, 7, 9, 8)
BANDS = ((0, 8), (8, 12), (12, 16))
HALF = NZ // 2


def split_np(m):
    high = m.astype(ml_dtypes.bfloat16)
    low = (m - high.astype(np.float64)).astype(ml_dtypes.bfloat16)
    return high, low


def transforms():
    seen, reps = set(), []
    for u in range(N):
        for v in range(N):
            if (u, v) in seen:
                continue
            reps.append((u, v))
            seen.add((u, v))
            seen.add(((-u) % N, (-v) % N))
    u = np.array([r[0] for r in reps])[:, None]
    v = np.array([r[1] for r in reps])[:, None]
    weight = np.where((u == 0) & (v == 0), 1.0, 2.0) / N**2
    n = len(reps)

    def table(pos_j, pos_k, live, sign):
        angle = 2 * np.pi / N * (u * pos_j[None] + v * pos_k[None])
        out = np.zeros((2 * NF, len(pos_j)))
        out[:n] = np.cos(angle) * live
        out[NF : NF + n] = sign * np.sin(angle) * live
        return out

    scale = np.zeros((2 * NF, 1))
    scale[:n] = weight
    scale[NF : NF + n] = weight
    cell = np.arange(G * G)
    tap = np.arange(8 * W)
    live = ((tap % 8) < W)[None]
    fwd = table(cell // G, cell % G, 1.0, -1.0)
    inv = (fwd * scale).T
    ker = table(tap // 8 - 3, tap % 8 - 3, live, 1.0)
    lag = (table(tap // 8 - 3, tap % 8 - 3, live, -1.0) * scale).T
    return tuple(np.concatenate(split_np(m), axis=0) for m in (fwd, ker, inv, lag))


def dot(a, b):
    return jnp.dot(a, b, preferred_element_type=F32)


def dot_nt(a, b):
    return lax.dot_general(a, b, (((1,), (1,)), ((), ())), preferred_element_type=F32)


def dot_tn(a, b):
    return lax.dot_general(a, b, (((0,), (0,)), ((), ())), preferred_element_type=F32)


def halves(value):
    high = value.astype(BF)
    return high, (value - high.astype(F32)).astype(BF)


def dot3(m, value):
    high, low = halves(value)
    rows = m.shape[0] // 2
    both = dot(m, high)
    return both[:rows] + both[rows:] + dot(m[:rows], low)


def kernel_body(
    x_hbm, cot_hbm, ker_hbm, bdw_hbm, gain_hbm, bias_hbm, win_hbm, bin_hbm, wout_hbm, bout_hbm,
    gamma_hbm, fm_hbm, km_hbm, im_hbm, lm_hbm,
    out_ref, dx_ref, dker_ref, vbdw_ref, vgain_ref, vbias_ref, dwi_ref, dbi_ref, dwo_ref,
    vbout_ref, vgamma_ref,
    x_ref, cot_ref, ker_ref, bdw_ref, gain_ref, bias_ref, win_ref, bin_ref, wout_ref, bout_ref,
    gamma_ref, fm_ref, km_ref, im_ref, lm_ref, l_sem, blk_ref,
    halo_x, halo_d, wall, swall, r1, t1, t1b, r2, t2, t2b, r3,
    kpad, kf, xf, df, yf, gf, mixed, na, dba, branch, dnorm, dmb,
    pay, payb, rx, zt, ztb, rz, agz, fin, wrk, hid, dpb,
    s_halo, q_halo, s_ga, q_ga, s_gb, q_gb, s_gc, q_gc, s_hd, q_hd,
    s_rc, q_rc, s_rb, q_rb, s_ra, q_ra, s_px, q_px, s_pz, q_pz, s_az, q_az, s_ax, q_ax,
):
    scale = float(NS * CELLS) ** (-0.5)
    s = lax.axis_index("space")
    core = lax.rem(s, 2)
    z = lax.rem(s // 2, NZ)
    x = s // (2 * NZ)

    def place(px, pz, pc):
        return {"space": (px * NZ + pz) * 2 + pc}

    def at_z(d):
        return place(x, lax.rem(z + d + NZ, NZ), core)

    def at_x(d):
        return place(lax.rem(x + d + NX, NX), z, core)

    def at_xc(k):
        return place(lax.rem(x + k % NX, NX), z, core if k < NX else 1 - core)

    partner = place(x, z, 1 - core)
    right = {"space": lax.rem(s + 1, NS)}
    left = {"space": lax.rem(s + NS - 1, NS)}

    def copy(src, dst, ssem, rsem, dev):
        return pltpu.make_async_remote_copy(
            src_ref=src, dst_ref=dst, send_sem=ssem, recv_sem=rsem, device_id=dev, device_id_type=MESH
        )

    pending = []

    def launch(copies):
        for c in copies:
            c.start()
        pending.extend(copies)
        return copies

    def flush():
        for c in pending:
            c.wait_send()
        pending.clear()

    def arrive(copies):
        for c in copies:
            c.wait_recv()

    barrier = pltpu.get_barrier_semaphore()
    peers = [at_z(d) for d in ORDER[:0:-1]] + [at_xc(k) for k in range(1, 2 * NX)] + [left, right]
    for dev in peers:
        pl.semaphore_signal(barrier, inc=1, device_id=dev, device_id_type=MESH)
    pairs = [
        (win_hbm, win_ref), (bin_hbm, bin_ref), (wout_hbm, wout_ref), (ker_hbm, ker_ref),
        (km_hbm, km_ref), (fm_hbm, fm_ref), (x_hbm, x_ref), (im_hbm, im_ref), (bdw_hbm, bdw_ref),
        (gain_hbm, gain_ref), (bias_hbm, bias_ref), (cot_hbm, cot_ref), (gamma_hbm, gamma_ref),
        (bout_hbm, bout_ref), (lm_hbm, lm_ref),
    ]
    loads = [pltpu.make_async_copy(a, b, l_sem.at[i]) for i, (a, b) in enumerate(pairs)]
    for c in loads:
        c.start()

    for c in loads[:3]:
        c.wait()
    row = lax.broadcasted_iota(jnp.int32, (8, 128), 0)
    col = lax.broadcasted_iota(jnp.int32, (8, 128), 1)
    wrk[...] = jnp.zeros_like(wrk)
    wrk[0:UNITS, 0:C] = win_ref[...].astype(F32)
    wrk[0:UNITS, 256:LANES] = wout_ref[:, 0:128].astype(F32)
    wrk[0:UNITS, C:256] = wout_ref[:, 128:C].astype(F32)
    wrk[UNITS : UNITS + 1, 0:UNITS] = bin_ref[...].astype(F32)
    blk_ref[...] = wrk[...].astype(BF)
    pl.semaphore_wait(barrier, len(peers))

    gather_a = launch([
        copy(blk_ref, wall.at[0, 0, i], s_ga.at[i - 1], q_ga.at[i - 1], at_z(ORDER[i]))
        for i in range(NZ - 1, 0, -1)
    ])[::-1]
    halo = launch([
        copy(x_hbm.at[pl.ds(64, 192)], halo_x.at[0], s_halo.at[0], q_halo.at[0], right),
        copy(x_hbm.at[pl.ds(0, 192)], halo_x.at[1], s_halo.at[1], q_halo.at[1], left),
    ])
    wall[0, 0, 0] = blk_ref[...]
    for c in loads[3:]:
        c.wait()

    kpad[...] = jnp.zeros_like(kpad)
    for a in range(W):
        for b in range(W):
            kpad[a, 8 * b : 8 * b + W, :] = ker_ref[a, b]

    def transform(rows):
        both = dot(fm_ref[...], rows)
        return both[: 2 * NF] + both[2 * NF :]

    km = km_ref[...]

    def ker_step(a, carry):
        kf[a] = dot3(km, kpad[a])
        return carry

    lax.fori_loop(0, W, ker_step, 0)
    for p in range(SX):
        xf[3 + p] = transform(x_ref[64 * p : 64 * p + 64, :])

    arrive(halo)
    has_left = (s > 0).astype(F32)
    has_right = (s < NS - 1).astype(F32)
    for p in range(3):
        xf[p] = transform(halo_x[0, 64 * p : 64 * p + 64, :]) * has_left
        xf[7 + p] = transform(halo_x[1, 64 * p : 64 * p + 64, :]) * has_right

    def forward_step(g, carry):
        top, low = pl.ds(pl.multiple_of(8 * g, 8), 8), pl.ds(pl.multiple_of(8 * g + NF, 8), 8)
        re = jnp.zeros((SX, 8, C), F32)
        im = jnp.zeros((SX, 8, C), F32)
        for a in range(W):
            kr, ki = kf[a, top, :], kf[a, low, :]
            xr, xi = xf[a : a + SX, top, :], xf[a : a + SX, low, :]
            re = re + kr * xr - ki * xi
            im = im + kr * xi + ki * xr
        yf[:, top, :] = re
        yf[:, low, :] = im
        return carry

    lax.fori_loop(0, NF // 8, forward_step, 0)
    inv = im_ref[...]
    for p in range(SX):
        mixed[64 * p : 64 * p + 64, :] = dot3(inv, yf[p]) + bdw_ref[...]

    mix = mixed[...]
    centred = mix - jnp.mean(mix, axis=-1, keepdims=True)
    inverse = lax.rsqrt(jnp.mean(centred * centred, axis=-1, keepdims=True) + 1e-06)
    unit = centred * inverse
    mixed[...] = unit
    lane = lax.broadcasted_iota(jnp.int32, (CELLS, 128), 1)
    na[:, 128:256] = jnp.where(lane == C - 128, 1.0, 0.0).astype(BF)
    na[:, 0:C] = (unit * gain_ref[...] + bias_ref[...]).astype(BF)
    d_branch = gamma_ref[...] * cot_ref[...].astype(F32)
    dba[:, 0:128] = jnp.zeros((CELLS, 128), BF)
    dba[:, 64:128] = d_branch[:, 128:C].astype(BF)
    dba[:, 128:256] = d_branch[:, 0:128].astype(BF)
    branch[...] = jnp.zeros_like(branch)
    dnorm[...] = jnp.zeros_like(dnorm)
    pay[...] = jnp.zeros_like(pay)
    gf[...] = jnp.zeros_like(gf)
    zt[pl.ds(CHUNK, NZ - CHUNK)] = jnp.zeros((NZ - CHUNK, 8, 128), F32)
    ztb[pl.ds(CHUNK, NZ - CHUNK)] = jnp.zeros((NZ - CHUNK, 8, 128), BF)
    v_bout = jnp.sum(d_branch, axis=0, keepdims=True)
    lane8 = lax.broadcasted_iota(jnp.int32, (2 * NZ, 8, 128), 2)
    row8 = lax.broadcasted_iota(jnp.int32, (2 * NZ, 8, 128), 1)

    gather_b, gather_c = {}, {}

    def band(dc, d, k):
        lo, hi = BANDS[k]
        return wall.at[dc, d, pl.ds(lo, hi - lo)]

    def pass_on(d, k):
        i = 3 * d + k
        gather_c[d, k] = launch([
            copy(band(0, d, k), band(1, d, k), s_gc.at[i], q_gc.at[i], partner)
        ])

    for k in range(3):
        lo, hi = BANDS[k]
        arrive(gather_a[max(lo, 1) - 1 : hi - 1])
        for d in (2, 1, 3):
            i = 3 * (d - 1) + k
            gather_b[d, k] = launch([
                copy(band(0, 0, k), band(0, d, k), s_gb.at[i], q_gb.at[i], at_x(d))
            ])
            if k == 2:
                i = 3 * d + k
                gather_c[d, k] = launch([
                    copy(band(0, 0, k), band(1, d, k), s_gc.at[i], q_gc.at[i], at_xc(NX + d))
                ])
        pass_on(0, k)

    def units(dc, i):
        block = wall[dc, :, pl.ds(HALF * i, HALF)].astype(F32).reshape(2 * NZ, 8, LANES)
        t_a, t_b = block[:, :, 0:128], block[:, :, 128:256]
        tail = jnp.broadcast_to(t_a[:, UNITS : UNITS + 1, :], t_a.shape)
        b_col = jnp.sum(jnp.where(row8 == lane8, tail, 0.0), axis=2, keepdims=True)
        t_bias = jnp.where(lane8 == C - 128, b_col, t_b)
        win = jnp.concatenate([t_a.reshape(256, 128), t_bias.reshape(256, 128)], axis=1).astype(BF)
        wout = block[:, :, 128:LANES].reshape(256, 256).astype(BF)
        normed, db = na[...], dba[...]
        pre = dot_nt(normed, win)
        half_erf = 0.5 * (1.0 + lax.erf(pre * root_half))
        hidden = (pre * half_erf).astype(BF)
        hid[dc, i] = hidden
        slope = half_erf + pre * jnp.exp(-0.5 * pre * pre) * inv_root_tau
        branch[...] += dot(hidden, wout)
        d_pre = (dot_nt(db, wout) * slope).astype(BF)
        dpb[dc, i] = d_pre
        dnorm[...] += dot(d_pre, win)

    def gradients(dc, i):
        part_of = pl.ds(HALF * i, HALF)
        hidden, d_pre, normed, db = hid[dc, i], dpb[dc, i], na[...], dba[...]
        dwi = (dot_tn(d_pre, normed) * scale).reshape(2 * NZ, 8, 256)
        dwo = (dot_tn(hidden, db) * scale).reshape(2 * NZ, 8, 256)
        g_a, g_b = dwi[:, :, 0:128], dwi[:, :, 128:256]
        g_col = jnp.broadcast_to(g_b[:, :, C - 128 : C - 127], g_b.shape)
        g_row = jnp.sum(jnp.where(row8 == lane8, g_col, 0.0), axis=1, keepdims=True)
        g_a = jnp.where(row8 == UNITS, jnp.broadcast_to(g_row, g_a.shape), g_a)
        g_b = jnp.where(lane8 < C - 128, g_b, dwo[:, :, 0:128])
        parts = (g_a, g_b, dwo[:, :, 128:256])
        for j, part in enumerate(parts):
            part = part.reshape(NX, HALF, 8, 128)
            if dc == 0:
                t1[:, part_of, :, 128 * j : 128 * j + 128] = part
            else:
                swall[:, part_of, :, 128 * j : 128 * j + 128] = part.astype(BF)

    def forward_on(k):
        for d in (1, 3, 2):
            arrive(gather_b[d, k])
            if k < 2:
                pass_on(d, k)

    def arrive_c(k):
        for d in range(NX):
            arrive(gather_c[d, k])

    forward_on(0)
    units(0, 0)
    forward_on(1)
    arrive_c(0)
    units(1, 0)
    forward_on(2)
    units(0, 1)
    arrive_c(1)
    arrive_c(2)
    units(1, 1)

    cot = cot_ref[...].astype(F32)
    full = jnp.concatenate([branch[:, 128:256], branch[:, 64:128]], axis=1) + bout_ref[...]
    v_gamma = jnp.sum(cot * full, axis=0, keepdims=True)

    dn = dnorm[:, 0:C]
    unit2 = mixed[...]
    v_gain = jnp.sum(dn * unit2, axis=0, keepdims=True)
    v_bias = jnp.sum(dn, axis=0, keepdims=True)
    scaled = dn * gain_ref[...]
    d_mixed = inverse * (
        scaled
        - jnp.mean(scaled, axis=-1, keepdims=True)
        - unit2 * jnp.mean(scaled * unit2, axis=-1, keepdims=True)
    )
    v_bdw = jnp.sum(d_mixed, axis=0, keepdims=True)
    dmb[...] = d_mixed.astype(BF)
    halo2 = launch([
        copy(dmb.at[pl.ds(64, 192)], halo_d.at[0], s_hd.at[0], q_hd.at[0], right),
        copy(dmb.at[pl.ds(0, 192)], halo_d.at[1], s_hd.at[1], q_hd.at[1], left),
    ])
    for p in range(SX):
        df[3 + p] = transform(dmb[64 * p : 64 * p + 64, :])

    def grad_step(g, carry):
        top, low = pl.ds(pl.multiple_of(8 * g, 8), 8), pl.ds(pl.multiple_of(8 * g + NF, 8), 8)
        dr, di = df[3 : 3 + SX, top, :], df[3 : 3 + SX, low, :]
        for a in range(W):
            xr, xi = xf[a : a + SX, top, :], xf[a : a + SX, low, :]
            gf[top, 256 * a : 256 * a + C] = jnp.sum(dr * xr + di * xi, axis=0)
            gf[low, 256 * a : 256 * a + C] = jnp.sum(dr * xi - di * xr, axis=0)
        return carry

    lax.fori_loop(0, NF // 8, grad_step, 0)
    lag = lm_ref[...]
    vectors = [v_bdw, v_gain, v_bias, v_bout, v_gamma]
    all_taps = dot3(lag, gf[...]) * scale
    for a in range(W):
        taps = all_taps[:, 256 * a : 256 * a + C]
        for b in range(W):
            group = a * W + b
            block = taps[8 * b : 8 * b + 8, :]
            q, t, r, u, at = spot(group)
            pay[q, t] = block[:, 0:128]
            pay[r, u, :, at : at + C - 128] = block[:, 128:C]
    for i, v in enumerate(vectors):
        q, t, r, u, at = spot(i)
        pay[q, t, W : W + 1, :] = v[:, 0:128] * scale
        pay[r, u, W : W + 1, at : at + C - 128] = v[:, 128:C] * scale
    payb[...] = pay[...].astype(BF)

    def chunk_of(k):
        px = lax.rem(x + k % NX, NX)
        pc = core if k < NX else 1 - core
        return pc * NX + px

    own = chunk_of(0)
    sum_x = launch([
        copy(payb.at[chunk_of(k)], rx.at[k - 1], s_px.at[k - 1], q_px.at[k - 1], at_xc(k))
        for k in range(1, 2 * NX)
    ])

    scatter_c = []
    for i in range(2):
        gradients(1, i)
        part_of = pl.ds(HALF * i, HALF)
        scatter_c += launch([
            copy(
                swall.at[d, part_of], r1.at[d, part_of], s_rc.at[NX * i + d], q_rc.at[NX * i + d],
                partner,
            )
            for d in range(NX)
        ])
    arrive(halo2)
    for p in range(3):
        df[p] = transform(halo_d[0, 64 * p : 64 * p + 64, :]) * has_left
        df[7 + p] = transform(halo_d[1, 64 * p : 64 * p + 64, :]) * has_right
    for i in range(2):
        gradients(0, i)
    arrive(scatter_c)

    def add_core(i, carry):
        total = t1[i] + r1[i].astype(F32)
        t1[i] = total
        t1b[i] = total.astype(BF)
        return carry

    lax.fori_loop(0, NX, add_core, 0)
    flush()
    scatter_b = launch([
        copy(t1b.at[d], r2.at[d - 1], s_rb.at[d - 1], q_rb.at[d - 1], at_x(-d)) for d in range(1, NX)
    ])

    arrive(sum_x)
    total = pay[own]
    for k in range(2 * NX - 1):
        total = total + rx[k].astype(F32)
    zt[pl.ds(0, CHUNK)] = total
    ztb[pl.ds(0, CHUNK)] = total.astype(BF)
    sum_z = launch([
        copy(
            ztb.at[lax.rem(z + ORDER[i], NZ)], rz.at[i - 1], s_pz.at[i - 1], q_pz.at[i - 1],
            at_z(ORDER[i]),
        )
        for i in range(NZ - 1, 0, -1)
    ])

    def back_step(g, carry):
        top, low = pl.ds(pl.multiple_of(8 * g, 8), 8), pl.ds(pl.multiple_of(8 * g + NF, 8), 8)
        re = jnp.zeros((SX, 8, C), F32)
        im = jnp.zeros((SX, 8, C), F32)
        for a in range(W):
            kr, ki = kf[W - 1 - a, top, :], kf[W - 1 - a, low, :]
            dr, di = df[a : a + SX, top, :], df[a : a + SX, low, :]
            re = re + kr * dr + ki * di
            im = im + kr * di - ki * dr
        yf[:, top, :] = re
        yf[:, low, :] = im
        return carry

    lax.fori_loop(0, NF // 8, back_step, 0)

    arrive(scatter_b)
    t2v = t1[0]
    for d in range(NX - 1):
        t2v = t2v + r2[d].astype(F32)
    t2[...] = t2v
    t2b[...] = t2v.astype(BF)
    flush()
    scatter_a = launch([
        copy(t2b.at[i], r3.at[i - 1], s_ra.at[i - 1], q_ra.at[i - 1], at_z(-ORDER[i]))
        for i in range(NZ - 1, 0, -1)
    ])

    arrive(sum_z)
    tile = zt[z]
    for i in range(NZ - 1):
        tile = tile + rz[i].astype(F32)
    agz[z] = tile.astype(BF)
    gather_z = launch([
        copy(agz.at[z], agz.at[z], s_az.at[i - 1], q_az.at[i - 1], at_z(ORDER[i]))
        for i in range(NZ - 1, 0, -1)
    ])

    full = jnp.concatenate([branch[:, 128:256], branch[:, 64:128]], axis=1) + bout_ref[...]
    out_ref[...] = (x_ref[...].astype(F32) + gamma_ref[...] * full).astype(BF)
    for p in range(SX):
        rows = slice(64 * p, 64 * p + 64)
        dx_ref[rows, :] = (cot_ref[rows, :].astype(F32) + dot3(inv, yf[p])).astype(BF)

    arrive(gather_z)
    fin[own] = agz[pl.ds(0, CHUNK)]
    gather_x = launch([
        copy(agz.at[pl.ds(0, CHUNK)], fin.at[own], s_ax.at[k - 1], q_ax.at[k - 1], at_xc(k)) for k in range(1, 2 * NX)
    ])

    arrive(scatter_a)
    mine = t2[0]
    for d in range(NZ - 1):
        mine = mine + r3[d].astype(F32)
    dwi_ref[...] = mine[0:UNITS, 0:C]
    dwo_ref[:, 0:128] = mine[0:UNITS, 256:LANES]
    dwo_ref[:, 128:C] = mine[0:UNITS, C:256]
    dbi_ref[...] = mine[UNITS : UNITS + 1, 0:UNITS]

    arrive(gather_x)
    for group in range(W * W):
        q, t, r, u, at = spot(group)
        first, second = fin[q, t].astype(F32), fin[r, u].astype(F32)[:, at : at + C - 128]
        dker_ref[group // W, group % W, :, 0:128] = first[0:W]
        dker_ref[group // W, group % W, :, 128:C] = second[0:W]
        if group < 5:
            v_ref = (vbdw_ref, vgain_ref, vbias_ref, vbout_ref, vgamma_ref)[group]
            v_ref[:, 0:128] = first[W : W + 1]
            v_ref[:, 128:C] = second[W : W + 1]

    flush()


def spot(group):
    first = 3 * (group // 2)
    whole, part = first + group % 2, first + 2
    return whole // CHUNK, whole % CHUNK, part // CHUNK, part % CHUNK, (C - 128) * (group % 2)


def emit_body(*refs):
    n = (len(refs) - 1) // 2
    sems = refs[-1]
    copies = [pltpu.make_async_copy(refs[i], refs[n + i], sems.at[i]) for i in range(n)]
    for c in copies:
        c.start()
    for c in copies:
        c.wait()


def on_device(
    features, cotangent, kernel, b_dw, ln_gain, ln_bias, w_in_t, b_in, w_out, b_out, gamma
):
    operands = [
        features.reshape(CELLS, C), cotangent.reshape(CELLS, C), kernel,
        b_dw.reshape(1, C), ln_gain.reshape(1, C), ln_bias.reshape(1, C), w_in_t,
        b_in.reshape(1, UNITS), w_out, b_out.reshape(1, C), gamma.reshape(1, C),
    ] + [jnp.asarray(m) for m in transforms()]
    vm = pl.BlockSpec(memory_space=pltpu.VMEM)
    hbm = pl.BlockSpec(memory_space=pltpu.HBM)
    dma = pltpu.SemaphoreType.DMA
    counts = [2, NZ - 1, 9, 12, 2, 2 * NX, NX - 1, NZ - 1, 2 * NX - 1, NZ - 1, NZ - 1, 2 * NX - 1]
    sems = [dma((n,)) for n in counts for _ in range(2)]
    scratch = [pltpu.VMEM(o.shape, o.dtype) for o in operands] + [
        dma((len(operands),)),
        pltpu.VMEM((8, LANES), BF),
        pltpu.VMEM((2, 192, C), BF),
        pltpu.VMEM((2, 192, C), BF),
        pltpu.VMEM((2, NX, NZ, 8, LANES), BF),
        pltpu.VMEM((NX, NZ, 8, LANES), BF),
        pltpu.VMEM((NX, NZ, 8, LANES), BF),
        pltpu.VMEM((NX, NZ, 8, LANES), F32),
        pltpu.VMEM((NX, NZ, 8, LANES), BF),
        pltpu.VMEM((NX - 1, NZ, 8, LANES), BF),
        pltpu.VMEM((NZ, 8, LANES), F32),
        pltpu.VMEM((NZ, 8, LANES), BF),
        pltpu.VMEM((NZ - 1, 8, LANES), BF),
        pltpu.VMEM((W, 8 * W, C), F32),
        pltpu.VMEM((W, 2 * NF, C), F32),
        pltpu.VMEM((SX + 6, 2 * NF, C), F32),
        pltpu.VMEM((SX + 6, 2 * NF, C), F32),
        pltpu.VMEM((SX, 2 * NF, C), F32),
        pltpu.VMEM((2 * NF, 256 * W), F32),
        pltpu.VMEM((CELLS, C), F32),
        pltpu.VMEM((CELLS, 256), BF),
        pltpu.VMEM((CELLS, 256), BF),
        pltpu.VMEM((CELLS, 256), F32),
        pltpu.VMEM((CELLS, 256), F32),
        pltpu.VMEM((CELLS, C), BF),
        pltpu.VMEM((2 * NX, CHUNK, 8, 128), F32),
        pltpu.VMEM((2 * NX, CHUNK, 8, 128), BF),
        pltpu.VMEM((2 * NX - 1, CHUNK, 8, 128), BF),
        pltpu.VMEM((NZ, 8, 128), F32),
        pltpu.VMEM((NZ, 8, 128), BF),
        pltpu.VMEM((NZ - 1, 8, 128), BF),
        pltpu.VMEM((NZ, 8, 128), BF),
        pltpu.VMEM((2 * NX, CHUNK, 8, 128), BF),
        pltpu.VMEM((8, LANES), F32),
        pltpu.VMEM((2, 2, CELLS, 256), BF),
        pltpu.VMEM((2, 2, CELLS, 256), BF),
    ]
    vec = jax.ShapeDtypeStruct((1, C), F32)
    shapes = (
        jax.ShapeDtypeStruct((CELLS, C), BF),
        jax.ShapeDtypeStruct((CELLS, C), BF),
        jax.ShapeDtypeStruct((W, W, W, C), F32),
        vec, vec, vec,
        jax.ShapeDtypeStruct((UNITS, C), F32),
        jax.ShapeDtypeStruct((1, UNITS), F32),
        jax.ShapeDtypeStruct((UNITS, C), F32),
        vec, vec,
    )
    results = pl.pallas_call(
        kernel_body,
        out_shape=shapes,
        in_specs=[hbm] * len(operands),
        out_specs=(vm,) * len(shapes),
        scratch_shapes=scratch + sems,
        compiler_params=pltpu.CompilerParams(
            collective_id=0, has_side_effects=True, vmem_limit_bytes=48 * 1024 * 1024
        ),
    )(*[pltpu.with_memory_space_constraint(o, pltpu.HBM) for o in operands])
    results = pl.pallas_call(
        emit_body,
        out_shape=shapes,
        in_specs=[vm] * len(shapes),
        out_specs=(hbm,) * len(shapes),
        scratch_shapes=[dma((len(shapes),))],
    )(*[pltpu.with_memory_space_constraint(o, pltpu.VMEM) for o in results])
    out, dx, dker, bdw, gain, bias, dwi, dbi, dwo, bout, gam = results
    return (
        out.reshape(features.shape), dx.reshape(features.shape), dker,
        bdw.reshape(C), gain.reshape(C), bias.reshape(C), dwi, dbi.reshape(UNITS), dwo,
        bout.reshape(C), gam.reshape(C),
    )


def solution(mesh):
    cells = P(("crop", "space"), None, None, None)
    rows = P(("crop", "space"), None)
    in_specs = (
        cells, cells, P(), P(), P(), P(), P("space", None), P("space"), P("space", None), P(), P(),
    )
    out_specs = (
        cells, cells, P("crop", None, None, None), P("crop"), P("crop"), P("crop"),
        rows, P(("crop", "space")), rows, P("crop"), P("crop"),
    )
    return jax.shard_map(
        on_device, mesh=mesh, in_specs=in_specs, out_specs=out_specs, check_vma=False
    )
```

```python
import numpy as np
import jax
import jax.numpy as jnp
import ml_dtypes
from jax import lax
from jax.experimental import pallas as pl
from jax.experimental.pallas import tpu as pltpu
from jax.sharding import PartitionSpec as P

root_half = 0.7071067811865476
inv_root_tau = 0.3989422804014327
MESH = pl.DeviceIdType.MESH
F32 = jnp.float32
BF = jnp.bfloat16

NX, NZ, NS = 4, 16, 128
C = 192
W = 7
G = 8
SX = 4
CELLS = SX * G * G
N = 11
NF = 64
UNITS = 6
LANES = 384
CHUNK = 10
ORDER = (0, 1, 15, 2, 14, 3, 13, 4, 12, 5, 11, 6, 10, 7, 9, 8)
BANDS = ((0, 8), (8, 12), (12, 16))
HALF = NZ // 2


def split_np(m):
    high = m.astype(ml_dtypes.bfloat16)
    low = (m - high.astype(np.float64)).astype(ml_dtypes.bfloat16)
    return high, low


def transforms():
    seen, reps = set(), []
    for u in range(N):
        for v in range(N):
            if (u, v) in seen:
                continue
            reps.append((u, v))
            seen.add((u, v))
            seen.add(((-u) % N, (-v) % N))
    u = np.array([r[0] for r in reps])[:, None]
    v = np.array([r[1] for r in reps])[:, None]
    weight = np.where((u == 0) & (v == 0), 1.0, 2.0) / N**2
    n = len(reps)

    def table(pos_j, pos_k, live, sign):
        angle = 2 * np.pi / N * (u * pos_j[None] + v * pos_k[None])
        out = np.zeros((2 * NF, len(pos_j)))
        out[:n] = np.cos(angle) * live
        out[NF : NF + n] = sign * np.sin(angle) * live
        return out

    scale = np.zeros((2 * NF, 1))
    scale[:n] = weight
    scale[NF : NF + n] = weight
    cell = np.arange(G * G)
    tap = np.arange(8 * W)
    live = ((tap % 8) < W)[None]
    fwd = table(cell // G, cell % G, 1.0, -1.0)
    inv = (fwd * scale).T
    ker = table(tap // 8 - 3, tap % 8 - 3, live, 1.0)
    lag = (table(tap // 8 - 3, tap % 8 - 3, live, -1.0) * scale).T
    return tuple(np.concatenate(split_np(m), axis=0) for m in (fwd, ker, inv, lag))


def dot(a, b):
    return jnp.dot(a, b, preferred_element_type=F32)


def dot_nt(a, b):
    return lax.dot_general(a, b, (((1,), (1,)), ((), ())), preferred_element_type=F32)


def dot_tn(a, b):
    return lax.dot_general(a, b, (((0,), (0,)), ((), ())), preferred_element_type=F32)


def halves(value):
    high = value.astype(BF)
    return high, (value - high.astype(F32)).astype(BF)


def dot3(m, value):
    high, low = halves(value)
    rows = m.shape[0] // 2
    both = dot(m, high)
    return both[:rows] + both[rows:] + dot(m[:rows], low)


def kernel_body(
    x_hbm, cot_hbm, ker_hbm, bdw_hbm, gain_hbm, bias_hbm, win_hbm, bin_hbm, wout_hbm, bout_hbm,
    gamma_hbm, fm_hbm, km_hbm, im_hbm, lm_hbm,
    out_ref, dx_ref, dker_ref, vbdw_ref, vgain_ref, vbias_ref, dwi_ref, dbi_ref, dwo_ref,
    vbout_ref, vgamma_ref,
    x_ref, cot_ref, ker_ref, bdw_ref, gain_ref, bias_ref, win_ref, bin_ref, wout_ref, bout_ref,
    gamma_ref, fm_ref, km_ref, im_ref, lm_ref, l_sem, blk_ref,
    halo_x, halo_d, wall, swall, r1, t1, t1b, r2, t2, t2b, r3,
    kpad, kf, xf, df, yf, gf, mixed, na, dba, branch, dnorm, dmb,
    pay, payb, rx, zt, ztb, rz, agz, fin, wrk, hid, dpb,
    s_halo, q_halo, s_ga, q_ga, s_gb, q_gb, s_gc, q_gc, s_hd, q_hd,
    s_rc, q_rc, s_rb, q_rb, s_ra, q_ra, s_px, q_px, s_pz, q_pz, s_az, q_az, s_ax, q_ax,
):
    scale = float(NS * CELLS) ** (-0.5)
    s = lax.axis_index("space")
    core = lax.rem(s, 2)
    z = lax.rem(s // 2, NZ)
    x = s // (2 * NZ)

    def place(px, pz, pc):
        return {"space": (px * NZ + pz) * 2 + pc}

    def at_z(d):
        return place(x, lax.rem(z + d + NZ, NZ), core)

    def at_x(d):
        return place(lax.rem(x + d + NX, NX), z, core)

    def at_xc(k):
        return place(lax.rem(x + k % NX, NX), z, core if k < NX else 1 - core)

    partner = place(x, z, 1 - core)
    right = {"space": lax.rem(s + 1, NS)}
    left = {"space": lax.rem(s + NS - 1, NS)}

    def copy(src, dst, ssem, rsem, dev):
        return pltpu.make_async_remote_copy(
            src_ref=src, dst_ref=dst, send_sem=ssem, recv_sem=rsem, device_id=dev, device_id_type=MESH
        )

    pending = []

    def launch(copies):
        for c in copies:
            c.start()
        pending.extend(copies)
        return copies

    def flush():
        for c in pending:
            c.wait_send()
        pending.clear()

    def arrive(copies):
        for c in copies:
            c.wait_recv()

    barrier = pltpu.get_barrier_semaphore()
    peers = [at_z(d) for d in ORDER[:0:-1]] + [at_xc(k) for k in range(1, 2 * NX)] + [left, right]
    for dev in peers:
        pl.semaphore_signal(barrier, inc=1, device_id=dev, device_id_type=MESH)
    pairs = [
        (win_hbm, win_ref), (bin_hbm, bin_ref), (wout_hbm, wout_ref), (ker_hbm, ker_ref),
        (km_hbm, km_ref), (fm_hbm, fm_ref), (x_hbm, x_ref), (im_hbm, im_ref), (bdw_hbm, bdw_ref),
        (gain_hbm, gain_ref), (bias_hbm, bias_ref), (cot_hbm, cot_ref), (gamma_hbm, gamma_ref),
        (bout_hbm, bout_ref), (lm_hbm, lm_ref),
    ]
    loads = [pltpu.make_async_copy(a, b, l_sem.at[i]) for i, (a, b) in enumerate(pairs)]
    for c in loads:
        c.start()

    for c in loads[:3]:
        c.wait()
    row = lax.broadcasted_iota(jnp.int32, (8, 128), 0)
    col = lax.broadcasted_iota(jnp.int32, (8, 128), 1)
    wrk[...] = jnp.zeros_like(wrk)
    wrk[0:UNITS, 0:C] = win_ref[...].astype(F32)
    wrk[0:UNITS, 256:LANES] = wout_ref[:, 0:128].astype(F32)
    wrk[0:UNITS, C:256] = wout_ref[:, 128:C].astype(F32)
    wrk[UNITS : UNITS + 1, 0:UNITS] = bin_ref[...].astype(F32)
    blk_ref[...] = wrk[...].astype(BF)
    pl.semaphore_wait(barrier, len(peers))

    gather_a = launch([
        copy(blk_ref, wall.at[0, 0, i], s_ga.at[i - 1], q_ga.at[i - 1], at_z(ORDER[i]))
        for i in range(NZ - 1, 0, -1)
    ])[::-1]
    halo = launch([
        copy(x_hbm.at[pl.ds(64, 192)], halo_x.at[0], s_halo.at[0], q_halo.at[0], right),
        copy(x_hbm.at[pl.ds(0, 192)], halo_x.at[1], s_halo.at[1], q_halo.at[1], left),
    ])
    wall[0, 0, 0] = blk_ref[...]
    for c in loads[3:]:
        c.wait()

    kpad[...] = jnp.zeros_like(kpad)
    for a in range(W):
        for b in range(W):
            kpad[a, 8 * b : 8 * b + W, :] = ker_ref[a, b]

    def transform(rows):
        both = dot(fm_ref[...], rows)
        return both[: 2 * NF] + both[2 * NF :]

    km = km_ref[...]

    def ker_step(a, carry):
        kf[a] = dot3(km, kpad[a])
        return carry

    lax.fori_loop(0, W, ker_step, 0)
    for p in range(SX):
        xf[3 + p] = transform(x_ref[64 * p : 64 * p + 64, :])

    arrive(halo)
    has_left = (s > 0).astype(F32)
    has_right = (s < NS - 1).astype(F32)
    for p in range(3):
        xf[p] = transform(halo_x[0, 64 * p : 64 * p + 64, :]) * has_left
        xf[7 + p] = transform(halo_x[1, 64 * p : 64 * p + 64, :]) * has_right

    def forward_step(g, carry):
        top, low = pl.ds(pl.multiple_of(8 * g, 8), 8), pl.ds(pl.multiple_of(8 * g + NF, 8), 8)
        re = jnp.zeros((SX, 8, C), F32)
        im = jnp.zeros((SX, 8, C), F32)
        for a in range(W):
            kr, ki = kf[a, top, :], kf[a, low, :]
            xr, xi = xf[a : a + SX, top, :], xf[a : a + SX, low, :]
            re = re + kr * xr - ki * xi
            im = im + kr * xi + ki * xr
        yf[:, top, :] = re
        yf[:, low, :] = im
        return carry

    lax.fori_loop(0, NF // 8, forward_step, 0)
    inv = im_ref[...]
    for p in range(SX):
        mixed[64 * p : 64 * p + 64, :] = dot3(inv, yf[p]) + bdw_ref[...]

    mix = mixed[...]
    centred = mix - jnp.mean(mix, axis=-1, keepdims=True)
    inverse = lax.rsqrt(jnp.mean(centred * centred, axis=-1, keepdims=True) + 1e-06)
    unit = centred * inverse
    mixed[...] = unit
    lane = lax.broadcasted_iota(jnp.int32, (CELLS, 128), 1)
    na[:, 128:256] = jnp.where(lane == C - 128, 1.0, 0.0).astype(BF)
    na[:, 0:C] = (unit * gain_ref[...] + bias_ref[...]).astype(BF)
    d_branch = gamma_ref[...] * cot_ref[...].astype(F32)
    dba[:, 0:128] = jnp.zeros((CELLS, 128), BF)
    dba[:, 64:128] = d_branch[:, 128:C].astype(BF)
    dba[:, 128:256] = d_branch[:, 0:128].astype(BF)
    branch[...] = jnp.zeros_like(branch)
    dnorm[...] = jnp.zeros_like(dnorm)
    pay[...] = jnp.zeros_like(pay)
    gf[...] = jnp.zeros_like(gf)
    zt[pl.ds(CHUNK, NZ - CHUNK)] = jnp.zeros((NZ - CHUNK, 8, 128), F32)
    ztb[pl.ds(CHUNK, NZ - CHUNK)] = jnp.zeros((NZ - CHUNK, 8, 128), BF)
    v_bout = jnp.sum(d_branch, axis=0, keepdims=True)
    lane8 = lax.broadcasted_iota(jnp.int32, (2 * NZ, 8, 128), 2)
    row8 = lax.broadcasted_iota(jnp.int32, (2 * NZ, 8, 128), 1)

    gather_b, gather_c = {}, {}

    def band(dc, d, k):
        lo, hi = BANDS[k]
        return wall.at[dc, d, pl.ds(lo, hi - lo)]

    def pass_on(d, k):
        i = 3 * d + k
        gather_c[d, k] = launch([
            copy(band(0, d, k), band(1, d, k), s_gc.at[i], q_gc.at[i], partner)
        ])

    for k in range(3):
        lo, hi = BANDS[k]
        arrive(gather_a[max(lo, 1) - 1 : hi - 1])
        for d in (2, 1, 3):
            i = 3 * (d - 1) + k
            gather_b[d, k] = launch([
                copy(band(0, 0, k), band(0, d, k), s_gb.at[i], q_gb.at[i], at_x(d))
            ])
            if k == 2:
                i = 3 * d + k
                gather_c[d, k] = launch([
                    copy(band(0, 0, k), band(1, d, k), s_gc.at[i], q_gc.at[i], at_xc(NX + d))
                ])
        pass_on(0, k)

    def units(dc, i):
        block = wall[dc, :, pl.ds(HALF * i, HALF)].astype(F32).reshape(2 * NZ, 8, LANES)
        t_a, t_b = block[:, :, 0:128], block[:, :, 128:256]
        tail = jnp.broadcast_to(t_a[:, UNITS : UNITS + 1, :], t_a.shape)
        b_col = jnp.sum(jnp.where(row8 == lane8, tail, 0.0), axis=2, keepdims=True)
        t_bias = jnp.where(lane8 == C - 128, b_col, t_b)
        win = jnp.concatenate([t_a.reshape(256, 128), t_bias.reshape(256, 128)], axis=1).astype(BF)
        wout = block[:, :, 128:LANES].reshape(256, 256).astype(BF)
        normed, db = na[...], dba[...]
        pre = dot_nt(normed, win)
        half_erf = 0.5 * (1.0 + lax.erf(pre * root_half))
        hidden = (pre * half_erf).astype(BF)
        hid[dc, i] = hidden
        slope = half_erf + pre * jnp.exp(-0.5 * pre * pre) * inv_root_tau
        branch[...] += dot(hidden, wout)
        d_pre = (dot_nt(db, wout) * slope).astype(BF)
        dpb[dc, i] = d_pre
        dnorm[...] += dot(d_pre, win)

    def gradients(dc, i):
        part_of = pl.ds(HALF * i, HALF)
        hidden, d_pre, normed, db = hid[dc, i], dpb[dc, i], na[...], dba[...]
        dwi = (dot_tn(d_pre, normed) * scale).reshape(2 * NZ, 8, 256)
        dwo = (dot_tn(hidden, db) * scale).reshape(2 * NZ, 8, 256)
        g_a, g_b = dwi[:, :, 0:128], dwi[:, :, 128:256]
        g_col = jnp.broadcast_to(g_b[:, :, C - 128 : C - 127], g_b.shape)
        g_row = jnp.sum(jnp.where(row8 == lane8, g_col, 0.0), axis=1, keepdims=True)
        g_a = jnp.where(row8 == UNITS, jnp.broadcast_to(g_row, g_a.shape), g_a)
        g_b = jnp.where(lane8 < C - 128, g_b, dwo[:, :, 0:128])
        parts = (g_a, g_b, dwo[:, :, 128:256])
        for j, part in enumerate(parts):
            part = part.reshape(NX, HALF, 8, 128)
            if dc == 0:
                t1[:, part_of, :, 128 * j : 128 * j + 128] = part
            else:
                swall[:, part_of, :, 128 * j : 128 * j + 128] = part.astype(BF)

    def forward_on(k):
        for d in (1, 3, 2):
            arrive(gather_b[d, k])
            if k < 2:
                pass_on(d, k)

    def arrive_c(k):
        for d in range(NX):
            arrive(gather_c[d, k])

    forward_on(0)
    units(0, 0)
    forward_on(1)
    arrive_c(0)
    units(1, 0)
    forward_on(2)
    units(0, 1)
    arrive_c(1)
    arrive_c(2)
    units(1, 1)

    cot = cot_ref[...].astype(F32)
    full = jnp.concatenate([branch[:, 128:256], branch[:, 64:128]], axis=1) + bout_ref[...]
    v_gamma = jnp.sum(cot * full, axis=0, keepdims=True)

    dn = dnorm[:, 0:C]
    unit2 = mixed[...]
    v_gain = jnp.sum(dn * unit2, axis=0, keepdims=True)
    v_bias = jnp.sum(dn, axis=0, keepdims=True)
    scaled = dn * gain_ref[...]
    d_mixed = inverse * (
        scaled
        - jnp.mean(scaled, axis=-1, keepdims=True)
        - unit2 * jnp.mean(scaled * unit2, axis=-1, keepdims=True)
    )
    v_bdw = jnp.sum(d_mixed, axis=0, keepdims=True)
    dmb[...] = d_mixed.astype(BF)
    halo2 = launch([
        copy(dmb.at[pl.ds(64, 192)], halo_d.at[0], s_hd.at[0], q_hd.at[0], right),
        copy(dmb.at[pl.ds(0, 192)], halo_d.at[1], s_hd.at[1], q_hd.at[1], left),
    ])
    for p in range(SX):
        df[3 + p] = transform(dmb[64 * p : 64 * p + 64, :])

    def grad_step(g, carry):
        top, low = pl.ds(pl.multiple_of(8 * g, 8), 8), pl.ds(pl.multiple_of(8 * g + NF, 8), 8)
        dr, di = df[3 : 3 + SX, top, :], df[3 : 3 + SX, low, :]
        for a in range(W):
            xr, xi = xf[a : a + SX, top, :], xf[a : a + SX, low, :]
            gf[top, 256 * a : 256 * a + C] = jnp.sum(dr * xr + di * xi, axis=0)
            gf[low, 256 * a : 256 * a + C] = jnp.sum(dr * xi - di * xr, axis=0)
        return carry

    lax.fori_loop(0, NF // 8, grad_step, 0)
    lag = lm_ref[...]
    vectors = [v_bdw, v_gain, v_bias, v_bout, v_gamma]
    all_taps = dot3(lag, gf[...]) * scale
    for a in range(W):
        taps = all_taps[:, 256 * a : 256 * a + C]
        for b in range(W):
            group = a * W + b
            block = taps[8 * b : 8 * b + 8, :]
            q, t, r, u, at = spot(group)
            pay[q, t] = block[:, 0:128]
            pay[r, u, :, at : at + C - 128] = block[:, 128:C]
    for i, v in enumerate(vectors):
        q, t, r, u, at = spot(i)
        pay[q, t, W : W + 1, :] = v[:, 0:128] * scale
        pay[r, u, W : W + 1, at : at + C - 128] = v[:, 128:C] * scale
    payb[...] = pay[...].astype(BF)

    def chunk_of(k):
        px = lax.rem(x + k % NX, NX)
        pc = core if k < NX else 1 - core
        return pc * NX + px

    own = chunk_of(0)
    sum_x = launch([
        copy(payb.at[chunk_of(k)], rx.at[k - 1], s_px.at[k - 1], q_px.at[k - 1], at_xc(k))
        for k in range(1, 2 * NX)
    ])

    scatter_c = []
    for i in range(2):
        gradients(1, i)
        part_of = pl.ds(HALF * i, HALF)
        scatter_c += launch([
            copy(
                swall.at[d, part_of], r1.at[d, part_of], s_rc.at[NX * i + d], q_rc.at[NX * i + d],
                partner,
            )
            for d in range(NX)
        ])
    arrive(halo2)
    for p in range(3):
        df[p] = transform(halo_d[0, 64 * p : 64 * p + 64, :]) * has_left
        df[7 + p] = transform(halo_d[1, 64 * p : 64 * p + 64, :]) * has_right
    for i in range(2):
        gradients(0, i)
    arrive(scatter_c)

    def add_core(i, carry):
        total = t1[i] + r1[i].astype(F32)
        t1[i] = total
        t1b[i] = total.astype(BF)
        return carry

    lax.fori_loop(0, NX, add_core, 0)
    flush()
    scatter_b = launch([
        copy(t1b.at[d], r2.at[d - 1], s_rb.at[d - 1], q_rb.at[d - 1], at_x(-d)) for d in range(1, NX)
    ])

    arrive(sum_x)
    total = pay[own]
    for k in range(2 * NX - 1):
        total = total + rx[k].astype(F32)
    zt[pl.ds(0, CHUNK)] = total
    ztb[pl.ds(0, CHUNK)] = total.astype(BF)
    sum_z = launch([
        copy(
            ztb.at[lax.rem(z + ORDER[i], NZ)], rz.at[i - 1], s_pz.at[i - 1], q_pz.at[i - 1],
            at_z(ORDER[i]),
        )
        for i in range(NZ - 1, 0, -1)
    ])

    def back_step(g, carry):
        top, low = pl.ds(pl.multiple_of(8 * g, 8), 8), pl.ds(pl.multiple_of(8 * g + NF, 8), 8)
        re = jnp.zeros((SX, 8, C), F32)
        im = jnp.zeros((SX, 8, C), F32)
        for a in range(W):
            kr, ki = kf[W - 1 - a, top, :], kf[W - 1 - a, low, :]
            dr, di = df[a : a + SX, top, :], df[a : a + SX, low, :]
            re = re + kr * dr + ki * di
            im = im + kr * di - ki * dr
        yf[:, top, :] = re
        yf[:, low, :] = im
        return carry

    lax.fori_loop(0, NF // 8, back_step, 0)

    arrive(sum_z)
    tile = zt[z]
    for i in range(NZ - 1):
        tile = tile + rz[i].astype(F32)
    agz[z] = tile.astype(BF)
    gather_z = launch([
        copy(agz.at[z], agz.at[z], s_az.at[i - 1], q_az.at[i - 1], at_z(ORDER[i]))
        for i in range(NZ - 1, 0, -1)
    ])

    arrive(scatter_b)
    t2v = t1[0]
    for d in range(NX - 1):
        t2v = t2v + r2[d].astype(F32)
    t2[...] = t2v
    t2b[...] = t2v.astype(BF)
    flush()
    scatter_a = launch([
        copy(t2b.at[i], r3.at[i - 1], s_ra.at[i - 1], q_ra.at[i - 1], at_z(-ORDER[i]))
        for i in range(NZ - 1, 0, -1)
    ])

    full = jnp.concatenate([branch[:, 128:256], branch[:, 64:128]], axis=1) + bout_ref[...]
    out_ref[...] = (x_ref[...].astype(F32) + gamma_ref[...] * full).astype(BF)
    for p in range(SX):
        rows = slice(64 * p, 64 * p + 64)
        dx_ref[rows, :] = (cot_ref[rows, :].astype(F32) + dot3(inv, yf[p])).astype(BF)

    arrive(gather_z)
    fin[own] = agz[pl.ds(0, CHUNK)]
    gather_x = launch([
        copy(agz.at[pl.ds(0, CHUNK)], fin.at[own], s_ax.at[k - 1], q_ax.at[k - 1], at_xc(k)) for k in range(1, 2 * NX)
    ])

    arrive(scatter_a)
    mine = t2[0]
    for d in range(NZ - 1):
        mine = mine + r3[d].astype(F32)
    dwi_ref[...] = mine[0:UNITS, 0:C]
    dwo_ref[:, 0:128] = mine[0:UNITS, 256:LANES]
    dwo_ref[:, 128:C] = mine[0:UNITS, C:256]
    dbi_ref[...] = mine[UNITS : UNITS + 1, 0:UNITS]

    arrive(gather_x)
    for group in range(W * W):
        q, t, r, u, at = spot(group)
        first, second = fin[q, t].astype(F32), fin[r, u].astype(F32)[:, at : at + C - 128]
        dker_ref[group // W, group % W, :, 0:128] = first[0:W]
        dker_ref[group // W, group % W, :, 128:C] = second[0:W]
        if group < 5:
            v_ref = (vbdw_ref, vgain_ref, vbias_ref, vbout_ref, vgamma_ref)[group]
            v_ref[:, 0:128] = first[W : W + 1]
            v_ref[:, 128:C] = second[W : W + 1]

    flush()


def spot(group):
    first = 3 * (group // 2)
    whole, part = first + group % 2, first + 2
    return whole // CHUNK, whole % CHUNK, part // CHUNK, part % CHUNK, (C - 128) * (group % 2)


def emit_body(*refs):
    n = (len(refs) - 1) // 2
    sems = refs[-1]
    copies = [pltpu.make_async_copy(refs[i], refs[n + i], sems.at[i]) for i in range(n)]
    for c in copies:
        c.start()
    for c in copies:
        c.wait()


def on_device(
    features, cotangent, kernel, b_dw, ln_gain, ln_bias, w_in_t, b_in, w_out, b_out, gamma
):
    operands = [
        features.reshape(CELLS, C), cotangent.reshape(CELLS, C), kernel,
        b_dw.reshape(1, C), ln_gain.reshape(1, C), ln_bias.reshape(1, C), w_in_t,
        b_in.reshape(1, UNITS), w_out, b_out.reshape(1, C), gamma.reshape(1, C),
    ] + [jnp.asarray(m) for m in transforms()]
    vm = pl.BlockSpec(memory_space=pltpu.VMEM)
    hbm = pl.BlockSpec(memory_space=pltpu.HBM)
    dma = pltpu.SemaphoreType.DMA
    counts = [2, NZ - 1, 9, 12, 2, 2 * NX, NX - 1, NZ - 1, 2 * NX - 1, NZ - 1, NZ - 1, 2 * NX - 1]
    sems = [dma((n,)) for n in counts for _ in range(2)]
    scratch = [pltpu.VMEM(o.shape, o.dtype) for o in operands] + [
        dma((len(operands),)),
        pltpu.VMEM((8, LANES), BF),
        pltpu.VMEM((2, 192, C), BF),
        pltpu.VMEM((2, 192, C), BF),
        pltpu.VMEM((2, NX, NZ, 8, LANES), BF),
        pltpu.VMEM((NX, NZ, 8, LANES), BF),
        pltpu.VMEM((NX, NZ, 8, LANES), BF),
        pltpu.VMEM((NX, NZ, 8, LANES), F32),
        pltpu.VMEM((NX, NZ, 8, LANES), BF),
        pltpu.VMEM((NX - 1, NZ, 8, LANES), BF),
        pltpu.VMEM((NZ, 8, LANES), F32),
        pltpu.VMEM((NZ, 8, LANES), BF),
        pltpu.VMEM((NZ - 1, 8, LANES), BF),
        pltpu.VMEM((W, 8 * W, C), F32),
        pltpu.VMEM((W, 2 * NF, C), F32),
        pltpu.VMEM((SX + 6, 2 * NF, C), F32),
        pltpu.VMEM((SX + 6, 2 * NF, C), F32),
        pltpu.VMEM((SX, 2 * NF, C), F32),
        pltpu.VMEM((2 * NF, 256 * W), F32),
        pltpu.VMEM((CELLS, C), F32),
        pltpu.VMEM((CELLS, 256), BF),
        pltpu.VMEM((CELLS, 256), BF),
        pltpu.VMEM((CELLS, 256), F32),
        pltpu.VMEM((CELLS, 256), F32),
        pltpu.VMEM((CELLS, C), BF),
        pltpu.VMEM((2 * NX, CHUNK, 8, 128), F32),
        pltpu.VMEM((2 * NX, CHUNK, 8, 128), BF),
        pltpu.VMEM((2 * NX - 1, CHUNK, 8, 128), BF),
        pltpu.VMEM((NZ, 8, 128), F32),
        pltpu.VMEM((NZ, 8, 128), BF),
        pltpu.VMEM((NZ - 1, 8, 128), BF),
        pltpu.VMEM((NZ, 8, 128), BF),
        pltpu.VMEM((2 * NX, CHUNK, 8, 128), BF),
        pltpu.VMEM((8, LANES), F32),
        pltpu.VMEM((2, 2, CELLS, 256), BF),
        pltpu.VMEM((2, 2, CELLS, 256), BF),
    ]
    vec = jax.ShapeDtypeStruct((1, C), F32)
    shapes = (
        jax.ShapeDtypeStruct((CELLS, C), BF),
        jax.ShapeDtypeStruct((CELLS, C), BF),
        jax.ShapeDtypeStruct((W, W, W, C), F32),
        vec, vec, vec,
        jax.ShapeDtypeStruct((UNITS, C), F32),
        jax.ShapeDtypeStruct((1, UNITS), F32),
        jax.ShapeDtypeStruct((UNITS, C), F32),
        vec, vec,
    )
    results = pl.pallas_call(
        kernel_body,
        out_shape=shapes,
        in_specs=[hbm] * len(operands),
        out_specs=(vm,) * len(shapes),
        scratch_shapes=scratch + sems,
        compiler_params=pltpu.CompilerParams(
            collective_id=0, has_side_effects=True, vmem_limit_bytes=48 * 1024 * 1024
        ),
    )(*[pltpu.with_memory_space_constraint(o, pltpu.HBM) for o in operands])
    results = pl.pallas_call(
        emit_body,
        out_shape=shapes,
        in_specs=[vm] * len(shapes),
        out_specs=(hbm,) * len(shapes),
        scratch_shapes=[dma((len(shapes),))],
    )(*[pltpu.with_memory_space_constraint(o, pltpu.VMEM) for o in results])
    out, dx, dker, bdw, gain, bias, dwi, dbi, dwo, bout, gam = results
    return (
        out.reshape(features.shape), dx.reshape(features.shape), dker,
        bdw.reshape(C), gain.reshape(C), bias.reshape(C), dwi, dbi.reshape(UNITS), dwo,
        bout.reshape(C), gam.reshape(C),
    )


def solution(mesh):
    cells = P(("crop", "space"), None, None, None)
    rows = P(("crop", "space"), None)
    in_specs = (
        cells, cells, P(), P(), P(), P(), P("space", None), P("space"), P("space", None), P(), P(),
    )
    out_specs = (
        cells, cells, P("crop", None, None, None), P("crop"), P("crop"), P("crop"),
        rows, P(("crop", "space")), rows, P("crop"), P("crop"),
    )
    return jax.shard_map(
        on_device, mesh=mesh, in_specs=in_specs, out_specs=out_specs, check_vma=False
    )
```
